32 devices in a mesh: seq: 4 (over z), grp: 8 (over y, x, core).
Axes of the slice: x: 2, y: 2, z: 4, core: 2. Of those that a mesh axis runs over, the one named last changes fastest.
Arguments:
- tokens: bfloat16 [8, 512, 1024], P('grp', 'seq'), may hold values from -6 to 6
- segment_ids: int32 [8, 512], P('grp'), may hold values from 0 to 2, never falling along the last dimension, each value on 1 to 261 neighbouring positions
- cotangent: bfloat16 [8, 512, 1024], P('grp', 'seq'), may hold values from -6 to 6
- first_gain: bfloat16 [1024], P(('seq', 'grp')), may hold values from 0.5 to 1.5
- z_proj: bfloat16 [1024, 1536], P(('seq', 'grp')), may hold values from -0.1875 to 0.1875
- xbc_proj: bfloat16 [1024, 1792], P(('seq', 'grp')), may hold values from -0.1875 to 0.1875
- dt_proj: bfloat16 [1024, 24], P(('seq', 'grp')), may hold values from -0.1875 to 0.1875
- conv_weight: float32 [4, 1792], replicated, may hold values from -3 to 3
- conv_bias: float32 [1792], replicated, may hold values from -1.5 to 1.5
- dt_bias: float32 [24], replicated, may hold values from -5 to -3
- decay_log: float32 [24], replicated, may hold values from -4 to 1.5
- skip_gain: float32 [24], replicated, may hold values from 0.5 to 1.5
- ssm_gain: bfloat16 [1536], P(('seq', 'grp')), may hold values from 0.5 to 1.5
- ssm_out_proj: bfloat16 [1536, 1024], P(('seq', 'grp')), may hold values from -0.15625 to 0.15625
- q_proj: bfloat16 [1024, 512], P(('seq', 'grp')), may hold values from -1 to 1
- k_proj: bfloat16 [1024, 128], P(('seq', 'grp')), may hold values from -1 to 1
- v_proj: bfloat16 [1024, 128], P(('seq', 'grp')), may hold values from -0.1875 to 0.1875
- attn_out_proj: bfloat16 [512, 1024], P(('seq', 'grp')), may hold values from -1 to 1
- second_gain: bfloat16 [1024], P(('seq', 'grp')), may hold values from 0.5 to 1.5
- gate_proj: bfloat16 [1024, 2048], P(('seq', 'grp')), may hold values from -0.1875 to 0.1875
- up_proj: bfloat16 [1024, 2048], P(('seq', 'grp')), may hold values from -0.1875 to 0.1875
- down_proj: bfloat16 [2048, 1024], P(('seq', 'grp')), may hold values from -0.125 to 0.125
Outputs:
- block_out: bfloat16 [8, 512, 1024], P('grp', 'seq')
- tokens_grad: float32 [8, 512, 1024], P('grp', 'seq')
- first_gain_grad: float32 [1024], P(('seq', 'grp'))
- z_proj_grad: float32 [1024, 1536], P(('seq', 'grp'))
- xbc_proj_grad: float32 [1024, 1792], P(('seq', 'grp'))
- dt_proj_grad: float32 [1024, 24], P(('seq', 'grp'))
- conv_weight_grad: float32 [4, 1792], replicated
- conv_bias_grad: float32 [1792], replicated
- dt_bias_grad: float32 [24], replicated
- decay_log_grad: float32 [24], replicated
- skip_gain_grad: float32 [24], replicated
- ssm_gain_grad: float32 [1536], P(('seq', 'grp'))
- ssm_out_proj_grad: float32 [1536, 1024], P(('seq', 'grp'))
- q_proj_grad: float32 [1024, 512], P(('seq', 'grp'))
- k_proj_grad: float32 [1024, 128], P(('seq', 'grp'))
- v_proj_grad: float32 [1024, 128], P(('seq', 'grp'))
- attn_out_proj_grad: float32 [512, 1024], P(('seq', 'grp'))
- second_gain_grad: float32 [1024], P(('seq', 'grp'))
- gate_proj_grad: float32 [1024, 2048], P(('seq', 'grp'))
- up_proj_grad: float32 [1024, 2048], P(('seq', 'grp'))
- down_proj_grad: float32 [2048, 1024], P(('seq', 'grp'))
The draws below stay inside these ranges and needn't reach their ends.
Inputs may be any that keep to these rules, and one draw needn't show every extreme that they name: `segment_ids`: in each sequence the segment numbers start at 0 and never fall; a segment holds 1 to 261 tokens, and one holds exactly 261.
All inputs are finite; a program needn't handle non-finite values.
Results may differ from the reference program's by a relative error of at most 0.017.
The reference program's roundings to bfloat16 on the way count: a program that leaves them out, or rounds other values in their place, can miss the bound.
Values may be sent and summed in bfloat16 or wider, within the bound.
No kernel may reach another device: no remote copies, remote signals or barrier semaphores. Data moves between devices by JAX's collectives and lax.ppermute only.
A program may use at most 256 MiB of HBM per device.

```python
import math
import jax
import jax.numpy as jnp
import numpy as np
from jax import lax

D = 1024
FF = 2048
SSM_HEADS = 24
HEAD_DIM = 64
STATE = 128
CONV = 4
Q_HEADS = 8
KV_HEADS = 2
ATT_DIM = 64
SEG_COUNT = 3
SSM_DIM = 1536
CONV_DIM = 1792
SEQ_LEN = 512
SEQS = 8
SEG_MOST = 261


def draw_tokens(key, part):
    full_shape = (SEQS, SEQ_LEN, D)
    values = jnp.clip(jax.random.normal(jax.random.fold_in(key, 1), full_shape, jnp.float32), -6.0, 6.0)
    return values.astype(jnp.bfloat16)


def draw_q_proj(key, part):
    base_draw = jnp.clip(jax.random.normal(jax.random.fold_in(key, 2), (D, Q_HEADS * ATT_DIM), jnp.float32), -4.0, 4.0) * D ** (-0.5)
    return base_draw.astype(jnp.bfloat16)


def draw_k_proj(key, part):
    base_draw = jnp.clip(jax.random.normal(jax.random.fold_in(key, 3), (D, KV_HEADS * ATT_DIM), jnp.float32), -4.0, 4.0) * D ** (-0.5)
    return base_draw.astype(jnp.bfloat16)


def level_of(own_key, shape, cuts, least, high):
    level, own = 1.0, jax.random.fold_in(own_key, 6)
    for axis_at, shards_of in cuts:
        heights = jnp.exp(jax.random.uniform(jax.random.fold_in(own, axis_at), (shards_of,), jnp.float32, least / len(cuts), high / len(cuts)))
        level = level * jnp.repeat(heights, shape[axis_at] // shards_of).reshape([-1 if axis == axis_at else 1 for axis in range(len(shape))])
    return level


def profile(count, total, most, lean):
    loads = [(1 << 20) // math.isqrt(standing ** lean) + 1 for standing in range(2, count + 1)]
    rest, counts = total - most - (count - 1), [1] * (count - 1)
    while rest > 0:
        movable = [i for i in range(count - 1) if counts[i] < most]
        pool, budget = sum([loads[i] for i in movable]), rest
        for i in movable:
            extra = min(most - counts[i], max(1, budget * loads[i] // pool), rest)
            counts[i] = counts[i] + extra
            rest = rest - extra
    return np.array([most] + counts)


def ragged(own_key, number_of, total, bound, slope):
    if number_of == 2:
        one = jax.random.randint(own_key, (), max(1, total - bound), min(bound, total - 1) + 1)
        return jnp.stack([one, total - one])
    lengths = jnp.asarray(profile(number_of, total, bound, slope), jnp.int32)
    couples = (number_of - 1) // 2
    donor, taker = lengths[1:1 + 2 * couples:2], lengths[2:2 + 2 * couples:2]
    margin = jnp.minimum(donor - 1, bound - taker)
    moved = jax.random.randint(jax.random.fold_in(own_key, 1), (couples,), 0, 1 << 20) % (margin + 1)
    lengths = lengths.at[1:1 + 2 * couples:2].set(donor - moved).at[2:2 + 2 * couples:2].set(taker + moved)
    return lengths[jax.random.permutation(jax.random.fold_in(own_key, 2), number_of)]


def normal_values(stream_key, shape, width, most, cuts=(), held_as=jnp.bfloat16):
    factor_of = level_of(stream_key, shape, cuts, -0.22, 0.18) if cuts else 1.0
    array = jax.random.normal(stream_key, shape, jnp.float32) * width * factor_of
    return jnp.minimum(jnp.maximum(array, -most), most).astype(held_as)


def setup_inputs(seed: int = 0) -> dict:
    seeds = jax.random.split(jax.random.key(seed), 23)
    return {
        "tokens": draw_tokens(jax.random.fold_in(seeds[22], 71), 0),
        "segment_ids": jax.vmap(lambda own: jnp.searchsorted(jnp.cumsum(ragged(own, SEG_COUNT, SEQ_LEN, SEG_MOST, 0)), jnp.arange(SEQ_LEN), side="right"))(jax.random.split(seeds[1], SEQS)).reshape((SEQS, SEQ_LEN)).astype(jnp.int32),
        "cotangent": normal_values(seeds[2], (SEQS, SEQ_LEN, D), 1.0, 6.0, ((0, 8), (1, 4))),
        "first_gain": jnp.clip(1.0 + 0.1 * jax.random.normal(seeds[3], (D,), jnp.float32), 0.5, 1.5).astype(jnp.bfloat16),
        "z_proj": normal_values(seeds[4], (D, SSM_DIM), D ** -0.5, 0.1875, ((0, 32),)),
        "xbc_proj": normal_values(seeds[5], (D, CONV_DIM), D ** -0.5, 0.1875, ((0, 32),)),
        "dt_proj": normal_values(seeds[6], (D, SSM_HEADS), D ** -0.5, 0.1875, ((0, 32),)),
        "conv_weight": normal_values(seeds[7], (CONV, CONV_DIM), CONV ** -0.5, 3.0, (), jnp.float32),
        "conv_bias": normal_values(seeds[8], (CONV_DIM,), 0.3, 1.5, (), jnp.float32),
        "dt_bias": jnp.clip(jax.random.uniform(seeds[9], (SSM_HEADS,), jnp.float32, -5.0, -3.0), -5.0, -3.0),
        "decay_log": jnp.clip(jax.random.uniform(seeds[10], (SSM_HEADS,), jnp.float32, -4.0, 1.5), -4.0, 1.5),
        "skip_gain": jnp.clip(jax.random.uniform(seeds[11], (SSM_HEADS,), jnp.float32, 0.5, 1.5), 0.5, 1.5),
        "ssm_gain": jnp.clip(1.0 + 0.1 * jax.random.normal(seeds[12], (SSM_DIM,), jnp.float32), 0.5, 1.5).astype(jnp.bfloat16),
        "ssm_out_proj": normal_values(seeds[13], (SSM_DIM, D), SSM_DIM ** -0.5, 0.15625, ((0, 32),)),
        "q_proj": draw_q_proj(jax.random.fold_in(seeds[22], 71), 0),
        "k_proj": draw_k_proj(jax.random.fold_in(seeds[22], 71), 0),
        "v_proj": normal_values(seeds[16], (D, KV_HEADS * ATT_DIM), D ** -0.5, 0.1875, ((0, 32),)),
        "attn_out_proj": normal_values(seeds[17], (Q_HEADS * ATT_DIM, D), (ATT_DIM // 2) ** -0.5, 1.0, ((0, 32),)),
        "second_gain": jnp.clip(1.0 + 0.1 * jax.random.normal(seeds[18], (D,), jnp.float32), 0.5, 1.5).astype(jnp.bfloat16),
        "gate_proj": normal_values(seeds[19], (D, FF), D ** -0.5, 0.1875, ((0, 32),)),
        "up_proj": normal_values(seeds[20], (D, FF), D ** -0.5, 0.1875, ((0, 32),)),
        "down_proj": normal_values(seeds[21], (FF, D), FF ** -0.5, 0.125, ((0, 32),)),
    }


epsilon = 1e-05
att_scale = 0.125
highest = lax.Precision.HIGHEST

def rms_apply(values, gain):
    inverse = lax.rsqrt(lax.optimization_barrier(jnp.mean(values * values, axis=-1, keepdims=True)) + epsilon)
    return values * inverse * gain

def mat_dot(left, right):
    return jnp.dot(left, right, preferred_element_type=jnp.float32)

def swiglu_mix(gate_in, up_in):
    return jax.nn.silu(gate_in) * up_in

def ssm_prep(xbc_ext, dt_raw, conv_weight, conv_bias, dt_bias, decay_log, seg_ext):
    tok_rows = dt_raw.shape[0]
    seg_here = seg_ext[CONV - 1:]
    conv_total = jnp.zeros((tok_rows, xbc_ext.shape[1]), jnp.float32) + conv_bias[None, :]
    for lag_index in range(CONV):
        shifted = xbc_ext[lag_index:lag_index + tok_rows]
        same_seg = seg_ext[lag_index:lag_index + tok_rows] == seg_here
        conv_total = conv_total + jnp.where(same_seg[:, None], shifted, 0.0) * conv_weight[lag_index][None, :]
    activated = jax.nn.silu(conv_total)
    ssm_input = activated[:, :SSM_DIM]
    b_input = activated[:, SSM_DIM:SSM_DIM + STATE]
    c_input = activated[:, SSM_DIM + STATE:]
    step_size = jax.nn.softplus(dt_raw + dt_bias[None, :])
    log_decay = -step_size * jnp.exp(decay_log)[None, :]
    return (ssm_input, b_input, c_input, step_size, log_decay)

def ssm_output(ssm_input, b_input, c_input, step_size, log_decay, state_in, gate_z, skip_gain, ssm_gain, seg_here, carry_mask):
    tok_rows, head_count = step_size.shape
    inputs_h = ssm_input.reshape(tok_rows, head_count, HEAD_DIM)
    cumulative = jnp.cumsum(log_decay, axis=0)
    positions = jnp.arange(tok_rows)
    allowed = (seg_here[:, None] == seg_here[None, :]) & (positions[:, None] >= positions[None, :])
    allowed_h = allowed[:, :, None]
    spread = cumulative[:, None, :] - cumulative[None, :, :]
    weights_h = jnp.where(allowed_h, jnp.exp(jnp.where(allowed_h, spread, 0.0)), 0.0)
    intersection = jnp.dot(c_input, b_input.T, precision=highest)
    mixing = weights_h * intersection[:, :, None] * step_size[None, :, :]
    within = jnp.einsum('tsh,shp->thp', mixing, inputs_h, precision=highest)
    carried = jnp.einsum('tn,hpn->thp', c_input, state_in, precision=highest)
    carried = carried * (jnp.exp(cumulative) * carry_mask[:, None])[:, :, None]
    outputs_h = within + carried + skip_gain[None, :, None] * inputs_h
    gated = outputs_h.reshape(tok_rows, -1) * jax.nn.silu(gate_z)
    return rms_apply(gated, ssm_gain)

def attention_block(query_b, keys_b, values_b, query_pos, key_pos, query_seg, key_seg):
    q_rows = query_b.shape[0]
    k_rows = keys_b.shape[0]
    group = query_b.shape[1] // (KV_HEADS * ATT_DIM)
    query_h = query_b.reshape(q_rows, KV_HEADS, group, ATT_DIM).astype(jnp.float32)
    key_h = keys_b.reshape(k_rows, KV_HEADS, ATT_DIM).astype(jnp.float32)
    value_h = values_b.reshape(k_rows, KV_HEADS, ATT_DIM).astype(jnp.float32)
    scores = jnp.einsum('rkgd,ckd->kgrc', query_h, key_h) * att_scale
    allowed = (key_pos[None, :] <= query_pos[:, None]) & (key_seg[None, :] == query_seg[:, None])
    scores = jnp.where(allowed[None, None], scores, -1e+30)
    top_score = lax.optimization_barrier(jnp.max(scores, axis=-1, keepdims=True))
    total = lax.optimization_barrier(jnp.sum(jnp.exp(scores - top_score), axis=-1, keepdims=True))
    log_total = top_score + jnp.log(total)
    probs_b = jnp.exp(scores - log_total).astype(jnp.bfloat16)
    output = jnp.einsum('kgrc,ckd->rkgd', probs_b.astype(jnp.float32), value_h)
    return (output.reshape(q_rows, -1).astype(jnp.bfloat16), log_total[..., 0])

def attention_back(query_b, keys_b, values_b, out_b, log_total, grad_b, query_pos, key_pos, query_seg, key_seg):
    q_rows = query_b.shape[0]
    k_rows = keys_b.shape[0]
    group = query_b.shape[1] // (KV_HEADS * ATT_DIM)
    query_h = query_b.reshape(q_rows, KV_HEADS, group, ATT_DIM).astype(jnp.float32)
    key_h = keys_b.reshape(k_rows, KV_HEADS, ATT_DIM).astype(jnp.float32)
    value_h = values_b.reshape(k_rows, KV_HEADS, ATT_DIM).astype(jnp.float32)
    grad_h = grad_b.reshape(q_rows, KV_HEADS, group, ATT_DIM).astype(jnp.float32)
    out_h = out_b.reshape(q_rows, KV_HEADS, group, ATT_DIM).astype(jnp.float32)
    scores = jnp.einsum('rkgd,ckd->kgrc', query_h, key_h) * att_scale
    allowed = (key_pos[None, :] <= query_pos[:, None]) & (key_seg[None, :] == query_seg[:, None])
    scores = jnp.where(allowed[None, None], scores, -1e+30)
    probs = jnp.exp(scores - log_total[..., None])
    probs_b = probs.astype(jnp.bfloat16).astype(jnp.float32)
    delta = jnp.transpose(lax.optimization_barrier(jnp.sum(grad_h * out_h, axis=-1)), (1, 2, 0))
    prob_grad = jnp.einsum('rkgd,ckd->kgrc', grad_h, value_h)
    score_grad = (probs * (prob_grad - delta[..., None]) * att_scale).astype(jnp.bfloat16).astype(jnp.float32)
    query_grad = jnp.einsum('kgrc,ckd->rkgd', score_grad, key_h).reshape(q_rows, -1)
    key_grad = jnp.einsum('kgrc,rkgd->ckd', score_grad, query_h).reshape(k_rows, -1)
    value_grad = jnp.einsum('kgrc,rkgd->ckd', probs_b, grad_h).reshape(k_rows, -1)
    return (query_grad, key_grad, value_grad)

def reference(tokens, segment_ids, cotangent, first_gain, z_proj, xbc_proj, dt_proj, conv_weight, conv_bias, dt_bias, decay_log, skip_gain, ssm_gain, ssm_out_proj, q_proj, k_proj, v_proj, attn_out_proj, second_gain, gate_proj, up_proj, down_proj):
    seq_count, length, model_width = tokens.shape
    flat_tokens = tokens.reshape(seq_count * length, model_width).astype(jnp.float32)
    gain_first = first_gain.astype(jnp.float32)
    gain_second = second_gain.astype(jnp.float32)
    normed, norm_one_back = jax.vjp(rms_apply, flat_tokens, gain_first)
    normed_b = normed.astype(jnp.bfloat16)
    gate_z = mat_dot(normed_b, z_proj)
    xbc_b = mat_dot(normed_b, xbc_proj).astype(jnp.bfloat16)
    dt_raw = mat_dot(normed_b, dt_proj)
    query_b = mat_dot(normed_b, q_proj).astype(jnp.bfloat16)
    key_b = mat_dot(normed_b, k_proj).astype(jnp.bfloat16)
    value_b = mat_dot(normed_b, v_proj).astype(jnp.bfloat16)
    mixer_params = (conv_weight.astype(jnp.float32), conv_bias.astype(jnp.float32), dt_bias.astype(jnp.float32), decay_log.astype(jnp.float32), skip_gain.astype(jnp.float32), ssm_gain.astype(jnp.float32))
    positions = jnp.arange(length)

    def mixer_whole(xbc_rows, dt_rows, z_rows, seg_row, conv_w, conv_b, dt_b, decay_l, skip_g, ssm_g):
        pad_rows = CONV - 1
        xbc_ext = jnp.concatenate([jnp.zeros((pad_rows, xbc_rows.shape[1]), jnp.float32), xbc_rows], axis=0)
        seg_ext = jnp.concatenate([jnp.full((pad_rows,), -1, jnp.int32), seg_row.astype(jnp.int32)], axis=0)
        prepared = ssm_prep(xbc_ext, dt_rows, conv_w, conv_b, dt_b, decay_l, seg_ext)
        head_count = dt_rows.shape[1]
        state_zero = jnp.zeros((head_count, HEAD_DIM, STATE), jnp.float32)
        carry_zero = jnp.zeros((seg_row.shape[0],), jnp.float32)
        return ssm_output(*prepared, state_zero, z_rows, skip_g, ssm_g, seg_row, carry_zero)
    xbc_seq = xbc_b.astype(jnp.float32).reshape(seq_count, length, -1)
    dt_seq = dt_raw.reshape(seq_count, length, -1)
    z_seq = gate_z.reshape(seq_count, length, -1)
    query_seq = query_b.reshape(seq_count, length, -1)
    key_seq = key_b.reshape(seq_count, length, -1)
    value_seq = value_b.reshape(seq_count, length, -1)

    def forward_one(items):
        xbc_rows, dt_rows, z_rows, seg_row, query_rows, key_rows, value_rows = items
        mixed_rows = mixer_whole(xbc_rows, dt_rows, z_rows, seg_row, *mixer_params)
        attended_rows, log_rows = attention_block(query_rows, key_rows, value_rows, positions, positions, seg_row, seg_row)
        return (mixed_rows.astype(jnp.bfloat16), attended_rows, log_rows)
    mixed_seq, attended_seq, log_seq = lax.map(forward_one, (xbc_seq, dt_seq, z_seq, segment_ids, query_seq, key_seq, value_seq))
    mixed_b = mixed_seq.reshape(seq_count * length, -1)
    attended_b = attended_seq.reshape(seq_count * length, -1)
    resid = flat_tokens + mat_dot(mixed_b, ssm_out_proj) + mat_dot(attended_b, attn_out_proj)
    normed_two, norm_two_back = jax.vjp(rms_apply, resid, gain_second)
    normed_two_b = normed_two.astype(jnp.bfloat16)
    gate_val = mat_dot(normed_two_b, gate_proj)
    up_val = mat_dot(normed_two_b, up_proj)
    hidden, swiglu_back = jax.vjp(swiglu_mix, gate_val, up_val)
    hidden_b = hidden.astype(jnp.bfloat16)
    final = resid + mat_dot(hidden_b, down_proj)
    block_out = final.astype(jnp.bfloat16).reshape(tokens.shape)
    cot_b = cotangent.reshape(seq_count * length, model_width)
    down_proj_grad = mat_dot(hidden_b.T, cot_b)
    hidden_grad = mat_dot(cot_b, down_proj.T)
    gate_grad, up_grad = swiglu_back(hidden_grad)
    gate_grad_b = gate_grad.astype(jnp.bfloat16)
    up_grad_b = up_grad.astype(jnp.bfloat16)
    gate_proj_grad = mat_dot(normed_two_b.T, gate_grad_b)
    up_proj_grad = mat_dot(normed_two_b.T, up_grad_b)
    normed_two_grad = mat_dot(gate_grad_b, gate_proj.T) + mat_dot(up_grad_b, up_proj.T)
    resid_norm_grad, second_gain_grad = norm_two_back(normed_two_grad)
    resid_grad = cot_b.astype(jnp.float32) + resid_norm_grad
    resid_grad_b = resid_grad.astype(jnp.bfloat16)
    ssm_out_proj_grad = mat_dot(mixed_b.T, resid_grad_b)
    attn_out_proj_grad = mat_dot(attended_b.T, resid_grad_b)
    mixed_grad = mat_dot(resid_grad_b, ssm_out_proj.T)
    attended_grad_b = mat_dot(resid_grad_b, attn_out_proj.T).astype(jnp.bfloat16)
    mixed_grad_seq = mixed_grad.reshape(seq_count, length, -1)
    attended_grad_seq = attended_grad_b.reshape(seq_count, length, -1)

    def backward_one(carry, items):
        xbc_rows, dt_rows, z_rows, seg_row, query_rows, key_rows, value_rows, attended_rows, log_rows, mixed_grad_rows, attended_grad_rows = items

        def mixer_seq(xbc_in, dt_in, z_in, *params):
            return mixer_whole(xbc_in, dt_in, z_in, seg_row, *params)
        _, mixer_back = jax.vjp(mixer_seq, xbc_rows, dt_rows, z_rows, *mixer_params)
        mixer_grads = mixer_back(mixed_grad_rows)
        query_grad, key_grad, value_grad = attention_back(query_rows, key_rows, value_rows, attended_rows, log_rows, attended_grad_rows, positions, positions, seg_row, seg_row)
        new_carry = tuple((running + grad_item for running, grad_item in zip(carry, mixer_grads[3:])))
        return (new_carry, (mixer_grads[0], mixer_grads[1], mixer_grads[2], query_grad, key_grad, value_grad))
    carry_init = tuple((jnp.zeros_like(param_item) for param_item in mixer_params))
    sums, per_seq = lax.scan(backward_one, carry_init, (xbc_seq, dt_seq, z_seq, segment_ids, query_seq, key_seq, value_seq, attended_seq, log_seq, mixed_grad_seq, attended_grad_seq))
    xbc_grad_b = per_seq[0].reshape(seq_count * length, -1).astype(jnp.bfloat16)
    dt_grad_b = per_seq[1].reshape(seq_count * length, -1).astype(jnp.bfloat16)
    z_grad_b = per_seq[2].reshape(seq_count * length, -1).astype(jnp.bfloat16)
    query_grad_b = per_seq[3].reshape(seq_count * length, -1).astype(jnp.bfloat16)
    key_grad_b = per_seq[4].reshape(seq_count * length, -1).astype(jnp.bfloat16)
    value_grad_b = per_seq[5].reshape(seq_count * length, -1).astype(jnp.bfloat16)
    z_proj_grad = mat_dot(normed_b.T, z_grad_b)
    xbc_proj_grad = mat_dot(normed_b.T, xbc_grad_b)
    dt_proj_grad = mat_dot(normed_b.T, dt_grad_b)
    q_proj_grad = mat_dot(normed_b.T, query_grad_b)
    k_proj_grad = mat_dot(normed_b.T, key_grad_b)
    v_proj_grad = mat_dot(normed_b.T, value_grad_b)
    normed_grad = mat_dot(z_grad_b, z_proj.T) + mat_dot(xbc_grad_b, xbc_proj.T) + mat_dot(dt_grad_b, dt_proj.T)
    normed_grad = normed_grad + mat_dot(query_grad_b, q_proj.T) + mat_dot(key_grad_b, k_proj.T) + mat_dot(value_grad_b, v_proj.T)
    token_norm_grad, first_gain_grad = norm_one_back(normed_grad)
    tokens_grad = (resid_grad + token_norm_grad).reshape(tokens.shape)
    return (block_out, tokens_grad, first_gain_grad, z_proj_grad, xbc_proj_grad, dt_proj_grad, sums[0], sums[1], sums[2], sums[3], sums[4], sums[5], ssm_out_proj_grad, q_proj_grad, k_proj_grad, v_proj_grad, attn_out_proj_grad, second_gain_grad, gate_proj_grad, up_proj_grad, down_proj_grad)
```

```python
from functools import partial

import jax
import jax.numpy as jnp
from jax import lax
from jax.sharding import PartitionSpec as P

HEAD_DIM = 64
STATE = 128
CONV = 4
KV_HEADS = 2
ATT_DIM = 64
SSM_DIM = 1536


epsilon = 1e-05
att_scale = 0.125
highest = lax.Precision.HIGHEST


AXES = ("seq", "grp")


def shift(array, axis, by):
    length = lax.axis_size(axis)
    pairs = [(i, i + by) for i in range(length) if 0 <= i + by < length]
    return lax.ppermute(array, axis, pairs)


def device_count():
    return lax.axis_size("seq") * lax.axis_size("grp")


def device_bits():
    return device_count().bit_length() - 1


def device_bit(k):
    me = lax.axis_index("seq") * lax.axis_size("grp") + lax.axis_index("grp")
    return (me >> k) & 1


def swap(array, k):
    return lax.ppermute(array, AXES, [(i, i ^ (1 << k)) for i in range(device_count())])


def upward(array, k, down):
    senders = [i for i in range(device_count()) if ((i >> k) & 1) == (1 if down else 0)]
    return lax.ppermute(array, AXES, [(i, i ^ (1 << k)) for i in senders])


def order_of(color):
    bits = device_bits()
    low = list(range(1, bits - 1))
    by = color * len(low) // 3
    return low[by:] + low[:by] + [bits - 1]


def double(array, k, dim):
    other = swap(array, k)
    bit = device_bit(k)
    low = jnp.where(bit == 0, array, other)
    high = jnp.where(bit == 0, other, array)
    return jnp.concatenate([low, high], axis=dim)


def halve(array, k, dim):
    bit = device_bit(k)
    keep = lax.dynamic_index_in_dim(array, bit, dim, keepdims=True)
    send = lax.dynamic_index_in_dim(array, 1 - bit, dim, keepdims=True)
    return keep.astype(jnp.float32) + swap(send, k).astype(jnp.float32)


def gather_rows(piece, color):
    bits = device_bits()
    rows, width = piece.shape
    array = piece.reshape((1,) * bits + (rows, width))
    for k in order_of(color)[::-1] + [0]:
        array = double(array, k, bits - 1 - k)
    return array.reshape(device_count() * rows, width)


def scatter_rows(array, color):
    bits = device_bits()
    array = array.astype(jnp.bfloat16)
    order = order_of(color)
    for k in order:
        array = halve(array, k, bits - 1 - k)
        if k != order[-1]:
            array = array.astype(jnp.bfloat16)
    return array.reshape(array.shape[-2:])


def seq_bits():
    return lax.axis_size("seq").bit_length() - 1


def gather_seq(array):
    bits = seq_bits()
    base = device_bits() - bits
    rows, width = array.shape
    array = array.reshape((1,) * bits + (rows, width))
    for k in range(bits):
        array = double(array, base + k, bits - 1 - k)
    return array.reshape(-1, width)


def scatter_seq(array, rows):
    bits = seq_bits()
    base = device_bits() - bits
    array = array.reshape((2,) * bits + (rows, array.shape[-1]))
    for k in range(bits):
        array = halve(array.astype(jnp.bfloat16), base + k, bits - 1 - k)
    return array.reshape(rows, -1)


def own_half(array, rows, which):
    parts = array.reshape(array.shape[0], -1, 2, rows, *array.shape[2:])
    return lax.dynamic_index_in_dim(parts, which, 2, keepdims=False).reshape(array.shape[0], -1)


def pair_left(array, rows):
    bit = device_bit(0)
    mine = own_half(array, rows, bit)
    return mine, own_half(array, rows, 1 - bit)


def both(array):
    return jnp.concatenate([array, swap(array, 0)], axis=0)


def owners(array, rows):
    return array.reshape((2,) * (device_bits() - 1) + (1, rows, array.shape[-1]))


def thirds(array):
    width = array.shape[-1]
    step = -(-width // (3 * 128)) * 128
    return [array[..., i : min(i + step, width)] for i in range(0, width, step)]


def scan_states(decay, local, down):
    bits = seq_bits()
    base = device_bits() - bits
    heads, rows, width = local.shape

    def pack(decay, state):
        high = lax.reduce_precision(decay, 8, 7)
        low = decay - high
        extra = jnp.zeros((16, width), jnp.float32).at[0, :heads].set(high).at[1, :heads].set(low)
        return jnp.concatenate(
            [state.reshape(-1, width).astype(jnp.bfloat16), extra.astype(jnp.bfloat16)], axis=0
        )

    def unpack(buffer):
        wide = buffer.astype(jnp.float32)
        decay = wide[heads * rows, :heads] + wide[heads * rows + 1, :heads]
        return decay, wide[: heads * rows].reshape(heads, rows, width)

    ahead = (jnp.ones_like(decay), jnp.zeros_like(local))
    total = (decay, local)
    for k in range(bits):
        bit = device_bit(base + k)
        later = (bit == 0) if down else (bit == 1)
        buffer = pack(*total)
        last = k == bits - 1
        received = unpack(upward(buffer, base + k, down) if last else swap(buffer, base + k))
        joined = state_combine(received, ahead)
        ahead = jax.tree.map(lambda a, b: jnp.where(later, a, b), joined, ahead)
        if not last:
            first = jax.tree.map(lambda a, b: jnp.where(later, a, b), received, total)
            second = jax.tree.map(lambda a, b: jnp.where(later, b, a), received, total)
            total = state_combine(first, second)
    return ahead[1]


def rms_apply(values, gain):
    inverse = lax.rsqrt(jnp.mean(values * values, axis=-1, keepdims=True) + epsilon)
    return values * inverse * gain


def mat_dot(left, right):
    return jnp.dot(left, right, preferred_element_type=jnp.float32)


def trans_dot(left, right):
    return lax.dot_general(
        left, right, (((1,), (1,)), ((), ())), preferred_element_type=jnp.float32
    )


def row_contract(left, right):
    return lax.dot_general(
        left, right, (((0,), (0,)), ((), ())), preferred_element_type=jnp.float32
    )


def swiglu_mix(gate_in, up_in):
    return jax.nn.silu(gate_in) * up_in


def state_combine(earlier, later):
    return (earlier[0] * later[0], later[0][:, None, None] * earlier[1] + later[1])


def ssm_prep(xbc_ext, dt_raw, conv_weight, conv_bias, dt_bias, decay_log, seg_ext):
    tok_rows = dt_raw.shape[0]
    seg_here = seg_ext[CONV - 1 :]
    conv_total = jnp.zeros((tok_rows, xbc_ext.shape[1]), jnp.float32) + conv_bias[None, :]
    for lag_index in range(CONV):
        shifted = xbc_ext[lag_index : lag_index + tok_rows]
        same_seg = seg_ext[lag_index : lag_index + tok_rows] == seg_here
        conv_total = (
            conv_total
            + jnp.where(same_seg[:, None], shifted, 0.0) * conv_weight[lag_index][None, :]
        )
    activated = jax.nn.silu(conv_total)
    ssm_input = activated[:, :SSM_DIM]
    b_input = activated[:, SSM_DIM : SSM_DIM + STATE]
    c_input = activated[:, SSM_DIM + STATE :]
    step_size = jax.nn.softplus(dt_raw + dt_bias[None, :])
    log_decay = -step_size * jnp.exp(decay_log)[None, :]
    return (ssm_input, b_input, c_input, step_size, log_decay)


def ssm_output(
    ssm_input,
    b_input,
    c_input,
    step_size,
    log_decay,
    state_in,
    gate_z,
    skip_gain,
    ssm_gain,
    seg_here,
    carry_mask,
):
    tok_rows, head_count = step_size.shape
    inputs_h = ssm_input.reshape(tok_rows, head_count, HEAD_DIM)
    cumulative = jnp.cumsum(log_decay, axis=0)
    positions = jnp.arange(tok_rows)
    allowed = (seg_here[:, None] == seg_here[None, :]) & (positions[:, None] >= positions[None, :])
    allowed_h = allowed[:, :, None]
    spread = cumulative[:, None, :] - cumulative[None, :, :]
    weights_h = jnp.where(allowed_h, jnp.exp(jnp.where(allowed_h, spread, 0.0)), 0.0)
    intersection = jnp.dot(c_input, b_input.T, precision=highest)
    mixing = weights_h * intersection[:, :, None] * step_size[None, :, :]
    within = jnp.einsum("tsh,shp->thp", mixing, inputs_h, precision=highest)
    carried = jnp.einsum("tn,hpn->thp", c_input, state_in, precision=highest)
    carried = carried * (jnp.exp(cumulative) * carry_mask[:, None])[:, :, None]
    outputs_h = within + carried + skip_gain[None, :, None] * inputs_h
    gated = outputs_h.reshape(tok_rows, -1) * jax.nn.silu(gate_z)
    return rms_apply(gated, ssm_gain)


def ssm_state(ssm_input, b_input, step_size, log_decay, seg_here, carry_last):
    tok_rows, head_count = step_size.shape
    inputs_h = ssm_input.reshape(tok_rows, head_count, HEAD_DIM)
    cumulative = jnp.cumsum(log_decay, axis=0)
    final_sum = cumulative[-1]
    same_last = (seg_here == seg_here[-1]).astype(jnp.float32)
    weighting = jnp.exp(final_sum[None, :] - cumulative) * step_size * same_last[:, None]
    local_state = jnp.einsum("th,thp,tn->hpn", weighting, inputs_h, b_input, precision=highest)
    passing = jnp.exp(final_sum) * carry_last
    return (passing, local_state)


def attention_block(query_b, keys_b, values_b, query_pos, key_pos, query_seg, key_seg):
    q_rows = query_b.shape[0]
    k_rows = keys_b.shape[0]
    group = query_b.shape[1] // (KV_HEADS * ATT_DIM)
    query_h = query_b.reshape(q_rows, KV_HEADS, group, ATT_DIM)
    key_h = keys_b.reshape(k_rows, KV_HEADS, ATT_DIM)
    value_h = values_b.reshape(k_rows, KV_HEADS, ATT_DIM)
    scores = (
        jnp.einsum("rkgd,ckd->kgrc", query_h, key_h, preferred_element_type=jnp.float32) * att_scale
    )
    allowed = (key_pos[None, :] <= query_pos[:, None]) & (key_seg[None, :] == query_seg[:, None])
    scores = jnp.where(allowed[None, None], scores, -1e30)
    top_score = jnp.max(scores, axis=-1, keepdims=True)
    total = jnp.sum(jnp.exp(scores - top_score), axis=-1, keepdims=True)
    log_total = top_score + jnp.log(total)
    probs_b = jnp.exp(scores - log_total).astype(jnp.bfloat16)
    output = jnp.einsum("kgrc,ckd->rkgd", probs_b, value_h, preferred_element_type=jnp.float32)
    return (output.reshape(q_rows, -1).astype(jnp.bfloat16), log_total[..., 0])


def attention_back(
    query_b, keys_b, values_b, out_b, log_total, grad_b, query_pos, key_pos, query_seg, key_seg
):
    q_rows = query_b.shape[0]
    k_rows = keys_b.shape[0]
    group = query_b.shape[1] // (KV_HEADS * ATT_DIM)
    query_h = query_b.reshape(q_rows, KV_HEADS, group, ATT_DIM)
    key_h = keys_b.reshape(k_rows, KV_HEADS, ATT_DIM)
    value_h = values_b.reshape(k_rows, KV_HEADS, ATT_DIM)
    grad_h = grad_b.reshape(q_rows, KV_HEADS, group, ATT_DIM)
    out_h = out_b.reshape(q_rows, KV_HEADS, group, ATT_DIM)
    scores = (
        jnp.einsum("rkgd,ckd->kgrc", query_h, key_h, preferred_element_type=jnp.float32) * att_scale
    )
    allowed = (key_pos[None, :] <= query_pos[:, None]) & (key_seg[None, :] == query_seg[:, None])
    scores = jnp.where(allowed[None, None], scores, -1e30)
    probs = jnp.exp(scores - log_total[..., None])
    probs_b = probs.astype(jnp.bfloat16)
    delta = jnp.transpose(
        jnp.sum(grad_h.astype(jnp.float32) * out_h.astype(jnp.float32), axis=-1), (1, 2, 0)
    )
    prob_grad = jnp.einsum("rkgd,ckd->kgrc", grad_h, value_h, preferred_element_type=jnp.float32)
    score_grad = (probs * (prob_grad - delta[..., None]) * att_scale).astype(jnp.bfloat16)
    query_grad = jnp.einsum(
        "kgrc,ckd->rkgd", score_grad, key_h, preferred_element_type=jnp.float32
    ).reshape(q_rows, -1)
    key_grad = jnp.einsum(
        "kgrc,rkgd->ckd", score_grad, query_h, preferred_element_type=jnp.float32
    ).reshape(k_rows, -1)
    value_grad = jnp.einsum(
        "kgrc,rkgd->ckd", probs_b, grad_h, preferred_element_type=jnp.float32
    ).reshape(k_rows, -1)
    return (query_grad, key_grad, value_grad)


def shards(
    tokens,
    segment_ids,
    cotangent,
    first_gain,
    z_proj,
    xbc_proj,
    dt_proj,
    conv_weight,
    conv_bias,
    dt_bias,
    decay_log,
    skip_gain,
    ssm_gain,
    ssm_out_proj,
    q_proj,
    k_proj,
    v_proj,
    attn_out_proj,
    second_gain,
    gate_proj,
    up_proj,
    down_proj,
):
    seq_rank = lax.axis_index("seq")
    tok_rows = tokens.shape[1]
    length = segment_ids.shape[1]
    pad_rows = CONV - 1
    row_start = seq_rank * tok_rows
    seg_row = segment_ids[0]
    seg_padded = jnp.concatenate([jnp.full((pad_rows,), -1, jnp.int32), seg_row], axis=0)
    seg_ext = lax.dynamic_slice_in_dim(seg_padded, row_start, tok_rows + pad_rows)
    seg_here = seg_ext[pad_rows:]
    carry_mask = (seg_here == seg_ext[pad_rows - 1]).astype(jnp.float32)
    query_pos = row_start + jnp.arange(tok_rows)
    key_pos = jnp.arange(length)
    rows = z_proj.shape[0]
    out_rows, att_rows, down_rows = ssm_out_proj.shape[0], attn_out_proj.shape[0], down_proj.shape[0]
    width_d = tokens.shape[2]
    bc_width = xbc_proj.shape[1] - SSM_DIM
    gain_rows = ssm_gain.shape[0]
    gain_columns = -(-gain_rows // rows)
    heads = dt_proj.shape[1]
    ssm_gain_cols = jnp.pad(ssm_gain, (0, gain_columns * rows - gain_rows)).reshape(
        gain_columns, rows
    )
    tail_parts = [dt_proj, first_gain[:, None], second_gain[:, None], ssm_gain_cols.T]
    tail_width = sum(part.shape[1] for part in tail_parts)
    tail_pad = -tail_width % 128
    rest = jnp.concatenate(
        [xbc_proj[:, SSM_DIM:], q_proj, k_proj, v_proj, *tail_parts]
        + [jnp.zeros((rows, tail_pad), z_proj.dtype)],
        axis=1,
    )
    rest_full = gather_rows(rest, 0)
    x_full = gather_rows(xbc_proj[:, :SSM_DIM], 1)
    z_full = gather_rows(z_proj, 2)
    outs_local = jnp.concatenate([ssm_out_proj, attn_out_proj], axis=0)
    outs_local, gate_local, up_local, down_local, rest_full, x_full, z_full = (
        lax.optimization_barrier(
            (outs_local, gate_proj, up_proj, down_proj, rest_full, x_full, z_full)
        )
    )
    outs_full = [gather_rows(part, i) for i, part in enumerate(thirds(outs_local))]
    outs_full = [
        part.reshape(-1, out_rows + att_rows, part.shape[-1]) for part in outs_full
    ]
    ssm_out_full = jnp.concatenate(
        [part[:, :out_rows].reshape(-1, part.shape[-1]) for part in outs_full], axis=1
    )
    attn_out_full = jnp.concatenate(
        [part[:, out_rows:].reshape(-1, part.shape[-1]) for part in outs_full], axis=1
    )
    gate_full = gather_rows(gate_local, 0)
    up_full = gather_rows(up_local, 1)
    down_full = gather_rows(down_local, 2)
    q_width, k_width, v_width = q_proj.shape[1], k_proj.shape[1], v_proj.shape[1]
    q_at = bc_width
    k_at = q_at + q_width
    dt_at = k_at + k_width + v_width
    gain_at = dt_at + heads
    gain_one = rest_full[:, gain_at]
    gain_two = rest_full[:, gain_at + 1]
    ssm_gain_full = rest_full[:, gain_at + 2 : gain_at + 2 + gain_columns]
    ssm_gain_full = ssm_gain_full.reshape(-1, rows, gain_columns).transpose(0, 2, 1)
    ssm_gain_full = ssm_gain_full.reshape(-1, gain_columns * rows)[:, :gain_rows].reshape(-1)
    flat_tokens = tokens[0].astype(jnp.float32)
    normed, norm_one_back = jax.vjp(rms_apply, flat_tokens, gain_one.astype(jnp.float32))
    normed_b = normed.astype(jnp.bfloat16)
    rest_out = mat_dot(normed_b, rest_full)
    xbc_b = jnp.concatenate(
        [mat_dot(normed_b, x_full).astype(jnp.bfloat16), rest_out[:, :bc_width].astype(jnp.bfloat16)],
        axis=1,
    )
    gate_z = mat_dot(normed_b, z_full)
    query_b = rest_out[:, q_at:k_at].astype(jnp.bfloat16)
    kv_b = rest_out[:, k_at:dt_at].astype(jnp.bfloat16)
    dt_raw = rest_out[:, dt_at:gain_at]
    edge_rows = shift(xbc_b[tok_rows - pad_rows :], "seq", 1)
    xbc_ext = jnp.concatenate([edge_rows, xbc_b], axis=0).astype(jnp.float32)
    prepared, prep_back = jax.vjp(
        partial(ssm_prep, seg_ext=seg_ext),
        xbc_ext,
        dt_raw,
        conv_weight,
        conv_bias,
        dt_bias,
        decay_log,
    )
    ssm_input, b_input, c_input, step_size, log_decay = prepared
    state_parts, state_back = jax.vjp(
        partial(ssm_state, seg_here=seg_here, carry_last=carry_mask[-1]),
        ssm_input,
        b_input,
        step_size,
        log_decay,
    )
    passing, local_state = state_parts
    state_in = scan_states(passing, local_state, False)
    mixed, output_back = jax.vjp(
        partial(ssm_output, seg_here=seg_here, carry_mask=carry_mask),
        ssm_input,
        b_input,
        c_input,
        step_size,
        log_decay,
        state_in,
        gate_z,
        skip_gain,
        ssm_gain_full.astype(jnp.float32),
    )
    mixed_b = mixed.astype(jnp.bfloat16)
    kv_all = gather_seq(kv_b)
    kv_width = kv_b.shape[1] // 2
    keys_all, values_all = kv_all[:, :kv_width], kv_all[:, kv_width:]
    attended_b, log_total = attention_block(
        query_b, keys_all, values_all, query_pos, key_pos, seg_here, seg_row
    )
    resid = flat_tokens + mat_dot(mixed_b, ssm_out_full) + mat_dot(attended_b, attn_out_full)
    normed_two, norm_two_back = jax.vjp(rms_apply, resid, gain_two.astype(jnp.float32))
    normed_two_b = normed_two.astype(jnp.bfloat16)
    gate_val = mat_dot(normed_two_b, gate_full)
    up_val = mat_dot(normed_two_b, up_full)
    hidden, swiglu_back = jax.vjp(swiglu_mix, gate_val, up_val)
    hidden_b = hidden.astype(jnp.bfloat16)
    final = resid + mat_dot(hidden_b, down_full)
    block_out = final.astype(jnp.bfloat16)[None]
    cot_b = cotangent[0]
    cot_pair = both(cot_b)
    hidden_mine, hidden_other = pair_left(hidden_b, down_rows)
    down_proj_g = scatter_rows(
        owners(
            row_contract(jnp.concatenate([hidden_mine, swap(hidden_other, 0)], 0), cot_pair),
            down_rows,
        ),
        2,
    )
    hidden_grad = trans_dot(cot_b, down_full)
    gate_grad, up_grad = swiglu_back(hidden_grad)
    gate_grad_b = gate_grad.astype(jnp.bfloat16)
    up_grad_b = up_grad.astype(jnp.bfloat16)
    two_mine, two_other = pair_left(normed_two_b, rows)
    two_pair = jnp.concatenate([two_mine, swap(two_other, 0)], axis=0)
    gate_proj_g = scatter_rows(owners(row_contract(two_pair, both(gate_grad_b)), rows), 0)
    up_proj_g = scatter_rows(owners(row_contract(two_pair, both(up_grad_b)), rows), 1)
    normed_two_grad = trans_dot(gate_grad_b, gate_full) + trans_dot(up_grad_b, up_full)
    resid_norm_grad, second_gain_g = norm_two_back(normed_two_grad)
    resid_grad = cot_b.astype(jnp.float32) + resid_norm_grad
    resid_grad_b = resid_grad.astype(jnp.bfloat16)
    resid_pair = both(resid_grad_b)
    mixed_mine, mixed_other = pair_left(mixed_b, out_rows)
    att_mine, att_other = pair_left(attended_b, att_rows)
    outs_other = swap(jnp.concatenate([mixed_other, att_other], axis=1), 0)
    outs_pair = jnp.concatenate(
        [jnp.concatenate([mixed_mine, att_mine], axis=1), outs_other], axis=0
    )
    outs_g = row_contract(outs_pair, resid_pair)
    mixed_width = mixed_mine.shape[1]
    outs_g = jnp.concatenate(
        [owners(outs_g[:mixed_width], out_rows), owners(outs_g[mixed_width:], att_rows)], axis=-2
    )
    outs_g = jnp.concatenate(
        [scatter_rows(part, i) for i, part in enumerate(thirds(outs_g))], axis=-1
    )
    ssm_out_g, attn_out_g = outs_g[:out_rows], outs_g[out_rows:]
    mixed_grad = trans_dot(resid_grad_b, ssm_out_full)
    attended_grad_b = trans_dot(resid_grad_b, attn_out_full).astype(jnp.bfloat16)
    query_grad, key_part, value_part = attention_back(
        query_b,
        keys_all,
        values_all,
        attended_b,
        log_total,
        attended_grad_b,
        query_pos,
        key_pos,
        seg_here,
        seg_row,
    )
    kv_grad_b = scatter_seq(jnp.concatenate([key_part, value_part], axis=1), tok_rows).astype(
        jnp.bfloat16
    )
    (
        ga_input,
        ga_bvec,
        ga_cvec,
        ga_step,
        ga_decay,
        state_grad_local,
        z_grad,
        skip_gain_g,
        ssm_gain_g,
    ) = output_back(mixed_grad)
    later_grad = scan_states(passing, state_grad_local, True)
    passing_grad = jnp.sum(later_grad * state_in, axis=(1, 2))
    gb_input, gb_bvec, gb_step, gb_decay = state_back((passing_grad, later_grad))
    ext_grad, dt_raw_grad, conv_weight_g, conv_bias_g, dt_bias_g, decay_log_g = prep_back(
        (ga_input + gb_input, ga_bvec + gb_bvec, ga_cvec, ga_step + gb_step, ga_decay + gb_decay)
    )
    edge_grad = shift(ext_grad[:pad_rows], "seq", -1)
    xbc_grad = ext_grad[pad_rows:] + jnp.concatenate(
        [jnp.zeros((tok_rows - pad_rows, ext_grad.shape[1]), jnp.float32), edge_grad], axis=0
    )
    z_grad_b = z_grad.astype(jnp.bfloat16)
    xbc_grad_b = xbc_grad.astype(jnp.bfloat16)
    dt_grad_b = dt_raw_grad.astype(jnp.bfloat16)
    query_grad_b = query_grad.astype(jnp.bfloat16)
    rest_grad_b = jnp.concatenate(
        [xbc_grad_b[:, SSM_DIM:], query_grad_b, kv_grad_b, dt_grad_b]
        + [jnp.zeros((tok_rows, rest_full.shape[1] - gain_at), jnp.bfloat16)],
        axis=1,
    )
    x_grad_b = xbc_grad_b[:, :SSM_DIM]
    one_mine, one_other = pair_left(normed_b, rows)
    one_pair = jnp.concatenate([one_mine, swap(one_other, 0)], axis=0)
    z_proj_g = scatter_rows(owners(row_contract(one_pair, both(z_grad_b)), rows), 2)
    x_proj_g = scatter_rows(owners(row_contract(one_pair, both(x_grad_b)), rows), 1)
    rest_g = scatter_rows(owners(row_contract(one_pair, both(rest_grad_b)), rows), 0)
    xbc_proj_g = jnp.concatenate([x_proj_g, rest_g[:, :bc_width]], axis=1)
    normed_grad = (
        trans_dot(z_grad_b, z_full)
        + trans_dot(x_grad_b, x_full)
        + trans_dot(rest_grad_b, rest_full)
    )
    token_norm_grad, first_gain_g = norm_one_back(normed_grad)
    tokens_grad = (resid_grad + token_norm_grad)[None]
    small = jnp.concatenate(
        [
            conv_weight_g.reshape(-1),
            conv_bias_g,
            first_gain_g,
            second_gain_g,
            ssm_gain_g,
            dt_bias_g,
            decay_log_g,
            skip_gain_g,
        ]
    )
    sizes = [conv_weight_g.size, conv_bias_g.size, width_d, width_d, ssm_gain_g.size]
    sizes = sizes + [heads, heads, heads]
    small = jnp.pad(small, (0, -small.size % 1024)).reshape(-1, 1024)
    for k in range(device_bits()):
        small = small + swap(small, k)
    small = small.reshape(-1)
    ends = [sum(sizes[: i + 1]) for i in range(len(sizes))]
    cw, cb, g1, g2, gs, db, dl, sk = [small[e - s : e] for s, e in zip(sizes, ends)]
    me = seq_rank * lax.axis_size("grp") + lax.axis_index("grp")

    def mine(whole, count):
        return lax.dynamic_slice_in_dim(whole, me * count, count)

    return (
        block_out,
        tokens_grad,
        mine(g1, rows),
        z_proj_g,
        xbc_proj_g,
        rest_g[:, dt_at:gain_at],
        cw.reshape(conv_weight_g.shape),
        cb,
        db,
        dl,
        sk,
        mine(gs, gain_rows),
        ssm_out_g,
        rest_g[:, q_at:k_at],
        rest_g[:, k_at : k_at + k_width],
        rest_g[:, k_at + k_width : dt_at],
        attn_out_g,
        mine(g2, rows),
        gate_proj_g,
        up_proj_g,
        down_proj_g,
    )


def solution(mesh):
    in_specs = (
        P("grp", "seq", None),
        P("grp", None),
        P("grp", "seq", None),
        P(("seq", "grp")),
        P(("seq", "grp"), None),
        P(("seq", "grp"), None),
        P(("seq", "grp"), None),
        P(),
        P(),
        P(),
        P(),
        P(),
        P(("seq", "grp")),
        P(("seq", "grp"), None),
        P(("seq", "grp"), None),
        P(("seq", "grp"), None),
        P(("seq", "grp"), None),
        P(("seq", "grp"), None),
        P(("seq", "grp")),
        P(("seq", "grp"), None),
        P(("seq", "grp"), None),
        P(("seq", "grp"), None),
    )
    out_specs = (
        P("grp", "seq", None),
        P("grp", "seq", None),
        P(("seq", "grp")),
        P(("seq", "grp"), None),
        P(("seq", "grp"), None),
        P(("seq", "grp"), None),
        P(),
        P(),
        P(),
        P(),
        P(),
        P(("seq", "grp")),
        P(("seq", "grp"), None),
        P(("seq", "grp"), None),
        P(("seq", "grp"), None),
        P(("seq", "grp"), None),
        P(("seq", "grp"), None),
        P(("seq", "grp")),
        P(("seq", "grp"), None),
        P(("seq", "grp"), None),
        P(("seq", "grp"), None),
    )
    return jax.shard_map(shards, mesh=mesh, in_specs=in_specs, out_specs=out_specs, check_vma=False)
```

```python
from functools import partial

import jax
import jax.numpy as jnp
from jax import lax
from jax.sharding import PartitionSpec as P

HEAD_DIM = 64
STATE = 128
CONV = 4
KV_HEADS = 2
ATT_DIM = 64
SSM_DIM = 1536


epsilon = 1e-05
att_scale = 0.125
highest = lax.Precision.DEFAULT


AXES = ("seq", "grp")


def shift(array, axis, by):
    length = lax.axis_size(axis)
    pairs = [(i, i + by) for i in range(length) if 0 <= i + by < length]
    return lax.ppermute(array, axis, pairs)


def device_count():
    return lax.axis_size("seq") * lax.axis_size("grp")


def device_bits():
    return device_count().bit_length() - 1


def device_bit(k):
    me = lax.axis_index("seq") * lax.axis_size("grp") + lax.axis_index("grp")
    return (me >> k) & 1


def swap(array, k):
    return lax.ppermute(array, AXES, [(i, i ^ (1 << k)) for i in range(device_count())])


def upward(array, k, down):
    senders = [i for i in range(device_count()) if ((i >> k) & 1) == (1 if down else 0)]
    return lax.ppermute(array, AXES, [(i, i ^ (1 << k)) for i in senders])


def order_of(color):
    bits = device_bits()
    low = list(range(1, bits - 1))
    by = color * len(low) // 3
    return low[by:] + low[:by] + [bits - 1]


def double(array, k, dim):
    other = swap(array, k)
    bit = device_bit(k)
    low = jnp.where(bit == 0, array, other)
    high = jnp.where(bit == 0, other, array)
    return jnp.concatenate([low, high], axis=dim)


def halve(array, k, dim):
    bit = device_bit(k)
    keep = lax.dynamic_index_in_dim(array, bit, dim, keepdims=True)
    send = lax.dynamic_index_in_dim(array, 1 - bit, dim, keepdims=True)
    return keep.astype(jnp.float32) + swap(send, k).astype(jnp.float32)


def gather_rows(piece, color):
    bits = device_bits()
    rows, width = piece.shape
    array = piece.reshape((1,) * bits + (rows, width))
    for k in order_of(color)[::-1] + [0]:
        array = double(array, k, bits - 1 - k)
    return array.reshape(device_count() * rows, width)


class Scatter:
    def __init__(self, array, color):
        self.array = array.astype(jnp.bfloat16)
        self.order = order_of(color)

    def start(self):
        k = self.order.pop(0)
        dim, bit = device_bits() - 1 - k, device_bit(k)
        keep = lax.dynamic_index_in_dim(self.array, bit, dim, keepdims=True)
        send = lax.dynamic_index_in_dim(self.array, 1 - bit, dim, keepdims=True)
        return keep, swap(send, k)

    def finish(self, pending):
        keep, received = pending
        self.array = keep.astype(jnp.float32) + received.astype(jnp.float32)
        if self.order:
            self.array = self.array.astype(jnp.bfloat16)

    def result(self):
        while self.order:
            self.finish(self.start())
        return self.array.reshape(self.array.shape[-2:])


def advance(scatters, *others):
    pending = [scatter.start() for scatter in scatters]
    pending, others = lax.optimization_barrier((pending, others))
    for scatter, item in zip(scatters, pending):
        scatter.finish(item)
    return others


def seq_bits():
    return lax.axis_size("seq").bit_length() - 1


def gather_seq(array):
    bits = seq_bits()
    base = device_bits() - bits
    rows, width = array.shape
    array = array.reshape((1,) * bits + (rows, width))
    for k in range(bits):
        array = double(array, base + k, bits - 1 - k)
    return array.reshape(-1, width)


def scatter_seq(array, rows):
    bits = seq_bits()
    base = device_bits() - bits
    array = array.reshape((2,) * bits + (rows, array.shape[-1]))
    for k in range(bits):
        array = halve(array.astype(jnp.bfloat16), base + k, bits - 1 - k)
    return array.reshape(rows, -1)


def own_half(array, rows, which):
    parts = array.reshape(array.shape[0], -1, 2, rows, *array.shape[2:])
    return lax.dynamic_index_in_dim(parts, which, 2, keepdims=False).reshape(array.shape[0], -1)


def pair_left(array, rows):
    bit = device_bit(0)
    mine = own_half(array, rows, bit)
    return mine, own_half(array, rows, 1 - bit)


def both(array):
    return jnp.concatenate([array, swap(array, 0)], axis=0)


def owners(array, rows):
    return array.reshape((2,) * (device_bits() - 1) + (1, rows, array.shape[-1]))


def thirds(array):
    width = array.shape[-1]
    step = -(-width // (3 * 128)) * 128
    return [array[..., i : min(i + step, width)] for i in range(0, width, step)]


def scan_states(decay, local, down):
    bits = seq_bits()
    base = device_bits() - bits
    heads, rows, width = local.shape

    def pack(decay, state):
        high = lax.reduce_precision(decay, 8, 7)
        low = decay - high
        extra = jnp.zeros((16, width), jnp.float32).at[0, :heads].set(high).at[1, :heads].set(low)
        return jnp.concatenate(
            [state.reshape(-1, width).astype(jnp.bfloat16), extra.astype(jnp.bfloat16)], axis=0
        )

    def unpack(buffer):
        wide = buffer.astype(jnp.float32)
        decay = wide[heads * rows, :heads] + wide[heads * rows + 1, :heads]
        return decay, wide[: heads * rows].reshape(heads, rows, width)

    ahead = (jnp.ones_like(decay), jnp.zeros_like(local))
    total = (decay, local)
    for k in range(bits):
        bit = device_bit(base + k)
        later = (bit == 0) if down else (bit == 1)
        buffer = pack(*total)
        last = k == bits - 1
        received = unpack(upward(buffer, base + k, down) if last else swap(buffer, base + k))
        joined = state_combine(received, ahead)
        ahead = jax.tree.map(lambda a, b: jnp.where(later, a, b), joined, ahead)
        if not last:
            first = jax.tree.map(lambda a, b: jnp.where(later, a, b), received, total)
            second = jax.tree.map(lambda a, b: jnp.where(later, b, a), received, total)
            total = state_combine(first, second)
    return ahead[1]


def rms_apply(values, gain):
    inverse = lax.rsqrt(jnp.mean(values * values, axis=-1, keepdims=True) + epsilon)
    return values * inverse * gain


def mat_dot(left, right):
    return jnp.dot(left, right, preferred_element_type=jnp.float32)


def trans_dot(left, right):
    return lax.dot_general(
        left, right, (((1,), (1,)), ((), ())), preferred_element_type=jnp.float32
    )


def row_contract(left, right):
    return lax.dot_general(
        left, right, (((0,), (0,)), ((), ())), preferred_element_type=jnp.float32
    )


def swiglu_mix(gate_in, up_in):
    return jax.nn.silu(gate_in) * up_in


def state_combine(earlier, later):
    return (earlier[0] * later[0], later[0][:, None, None] * earlier[1] + later[1])


def ssm_prep(xbc_ext, dt_raw, conv_weight, conv_bias, dt_bias, decay_log, seg_ext):
    tok_rows = dt_raw.shape[0]
    seg_here = seg_ext[CONV - 1 :]
    conv_total = jnp.zeros((tok_rows, xbc_ext.shape[1]), jnp.float32) + conv_bias[None, :]
    for lag_index in range(CONV):
        shifted = xbc_ext[lag_index : lag_index + tok_rows]
        same_seg = seg_ext[lag_index : lag_index + tok_rows] == seg_here
        conv_total = (
            conv_total
            + jnp.where(same_seg[:, None], shifted, 0.0) * conv_weight[lag_index][None, :]
        )
    activated = jax.nn.silu(conv_total)
    ssm_input = activated[:, :SSM_DIM]
    b_input = activated[:, SSM_DIM : SSM_DIM + STATE]
    c_input = activated[:, SSM_DIM + STATE :]
    step_size = jax.nn.softplus(dt_raw + dt_bias[None, :])
    log_decay = -step_size * jnp.exp(decay_log)[None, :]
    return (ssm_input, b_input, c_input, step_size, log_decay)


def ssm_output(
    ssm_input,
    b_input,
    c_input,
    step_size,
    log_decay,
    state_in,
    gate_z,
    skip_gain,
    ssm_gain,
    seg_here,
    carry_mask,
):
    tok_rows, head_count = step_size.shape
    inputs_h = ssm_input.reshape(tok_rows, head_count, HEAD_DIM)
    cumulative = jnp.cumsum(log_decay, axis=0)
    positions = jnp.arange(tok_rows)
    allowed = (seg_here[:, None] == seg_here[None, :]) & (positions[:, None] >= positions[None, :])
    allowed_h = allowed[:, :, None]
    spread = cumulative[:, None, :] - cumulative[None, :, :]
    weights_h = jnp.where(allowed_h, jnp.exp(jnp.where(allowed_h, spread, 0.0)), 0.0)
    intersection = jnp.dot(c_input, b_input.T, precision=highest)
    mixing = weights_h * intersection[:, :, None] * step_size[None, :, :]
    within = jnp.einsum("tsh,shp->thp", mixing, inputs_h, precision=highest)
    carried = jnp.einsum("tn,hpn->thp", c_input, state_in, precision=highest)
    carried = carried * (jnp.exp(cumulative) * carry_mask[:, None])[:, :, None]
    outputs_h = within + carried + skip_gain[None, :, None] * inputs_h
    gated = outputs_h.reshape(tok_rows, -1) * jax.nn.silu(gate_z)
    return rms_apply(gated, ssm_gain)


def ssm_state(ssm_input, b_input, step_size, log_decay, seg_here, carry_last):
    tok_rows, head_count = step_size.shape
    inputs_h = ssm_input.reshape(tok_rows, head_count, HEAD_DIM)
    cumulative = jnp.cumsum(log_decay, axis=0)
    final_sum = cumulative[-1]
    same_last = (seg_here == seg_here[-1]).astype(jnp.float32)
    weighting = jnp.exp(final_sum[None, :] - cumulative) * step_size * same_last[:, None]
    local_state = jnp.einsum("th,thp,tn->hpn", weighting, inputs_h, b_input, precision=highest)
    passing = jnp.exp(final_sum) * carry_last
    return (passing, local_state)


def attention_block(query_b, keys_b, values_b, query_pos, key_pos, query_seg, key_seg):
    q_rows = query_b.shape[0]
    k_rows = keys_b.shape[0]
    group = query_b.shape[1] // (KV_HEADS * ATT_DIM)
    query_h = query_b.reshape(q_rows, KV_HEADS, group, ATT_DIM)
    key_h = keys_b.reshape(k_rows, KV_HEADS, ATT_DIM)
    value_h = values_b.reshape(k_rows, KV_HEADS, ATT_DIM)
    scores = (
        jnp.einsum("rkgd,ckd->kgrc", query_h, key_h, preferred_element_type=jnp.float32) * att_scale
    )
    allowed = (key_pos[None, :] <= query_pos[:, None]) & (key_seg[None, :] == query_seg[:, None])
    scores = jnp.where(allowed[None, None], scores, -1e30)
    top_score = jnp.max(scores, axis=-1, keepdims=True)
    total = jnp.sum(jnp.exp(scores - top_score), axis=-1, keepdims=True)
    log_total = top_score + jnp.log(total)
    probs_b = jnp.exp(scores - log_total).astype(jnp.bfloat16)
    output = jnp.einsum("kgrc,ckd->rkgd", probs_b, value_h, preferred_element_type=jnp.float32)
    return (output.reshape(q_rows, -1).astype(jnp.bfloat16), log_total[..., 0])


def attention_back(
    query_b, keys_b, values_b, out_b, log_total, grad_b, query_pos, key_pos, query_seg, key_seg
):
    q_rows = query_b.shape[0]
    k_rows = keys_b.shape[0]
    group = query_b.shape[1] // (KV_HEADS * ATT_DIM)
    query_h = query_b.reshape(q_rows, KV_HEADS, group, ATT_DIM)
    key_h = keys_b.reshape(k_rows, KV_HEADS, ATT_DIM)
    value_h = values_b.reshape(k_rows, KV_HEADS, ATT_DIM)
    grad_h = grad_b.reshape(q_rows, KV_HEADS, group, ATT_DIM)
    out_h = out_b.reshape(q_rows, KV_HEADS, group, ATT_DIM)
    scores = (
        jnp.einsum("rkgd,ckd->kgrc", query_h, key_h, preferred_element_type=jnp.float32) * att_scale
    )
    allowed = (key_pos[None, :] <= query_pos[:, None]) & (key_seg[None, :] == query_seg[:, None])
    scores = jnp.where(allowed[None, None], scores, -1e30)
    probs = jnp.exp(scores - log_total[..., None])
    probs_b = probs.astype(jnp.bfloat16)
    delta = jnp.transpose(
        jnp.sum(grad_h.astype(jnp.float32) * out_h.astype(jnp.float32), axis=-1), (1, 2, 0)
    )
    prob_grad = jnp.einsum("rkgd,ckd->kgrc", grad_h, value_h, preferred_element_type=jnp.float32)
    score_grad = (probs * (prob_grad - delta[..., None]) * att_scale).astype(jnp.bfloat16)
    query_grad = jnp.einsum(
        "kgrc,ckd->rkgd", score_grad, key_h, preferred_element_type=jnp.float32
    ).reshape(q_rows, -1)
    key_grad = jnp.einsum(
        "kgrc,rkgd->ckd", score_grad, query_h, preferred_element_type=jnp.float32
    ).reshape(k_rows, -1)
    value_grad = jnp.einsum(
        "kgrc,rkgd->ckd", probs_b, grad_h, preferred_element_type=jnp.float32
    ).reshape(k_rows, -1)
    return (query_grad, key_grad, value_grad)


def shards(
    tokens,
    segment_ids,
    cotangent,
    first_gain,
    z_proj,
    xbc_proj,
    dt_proj,
    conv_weight,
    conv_bias,
    dt_bias,
    decay_log,
    skip_gain,
    ssm_gain,
    ssm_out_proj,
    q_proj,
    k_proj,
    v_proj,
    attn_out_proj,
    second_gain,
    gate_proj,
    up_proj,
    down_proj,
):
    seq_rank = lax.axis_index("seq")
    tok_rows = tokens.shape[1]
    length = segment_ids.shape[1]
    pad_rows = CONV - 1
    row_start = seq_rank * tok_rows
    seg_row = segment_ids[0]
    seg_padded = jnp.concatenate([jnp.full((pad_rows,), -1, jnp.int32), seg_row], axis=0)
    seg_ext = lax.dynamic_slice_in_dim(seg_padded, row_start, tok_rows + pad_rows)
    seg_here = seg_ext[pad_rows:]
    carry_mask = (seg_here == seg_ext[pad_rows - 1]).astype(jnp.float32)
    query_pos = row_start + jnp.arange(tok_rows)
    key_pos = jnp.arange(length)
    rows = z_proj.shape[0]
    out_rows, att_rows, down_rows = ssm_out_proj.shape[0], attn_out_proj.shape[0], down_proj.shape[0]
    width_d = tokens.shape[2]
    bc_width = xbc_proj.shape[1] - SSM_DIM
    gain_rows = ssm_gain.shape[0]
    gain_columns = -(-gain_rows // rows)
    heads = dt_proj.shape[1]
    ssm_gain_cols = jnp.pad(ssm_gain, (0, gain_columns * rows - gain_rows)).reshape(
        gain_columns, rows
    )
    tail_parts = [dt_proj, first_gain[:, None], second_gain[:, None], ssm_gain_cols.T]
    tail_width = sum(part.shape[1] for part in tail_parts)
    tail_pad = -tail_width % 128
    rest = jnp.concatenate(
        [xbc_proj, q_proj, k_proj, v_proj, *tail_parts]
        + [jnp.zeros((rows, tail_pad), z_proj.dtype)],
        axis=1,
    )
    ff_width = gate_proj.shape[1] // width_d
    wide = [gate_proj[:, i * width_d : (i + 1) * width_d] for i in range(ff_width)]
    wide = wide + [up_proj[:, i * width_d : (i + 1) * width_d] for i in range(ff_width)]
    z_rows = rows * z_proj.shape[1] // width_d
    wide = wide + [down_proj, ssm_out_proj, attn_out_proj, z_proj.reshape(z_rows, width_d)]
    wide_full = lax.all_gather(jnp.concatenate(wide, axis=0), AXES)
    rest_full = jnp.concatenate(
        [gather_rows(part, i) for i, part in enumerate(thirds(rest))], axis=1
    )
    starts = [0]
    for part in wide:
        starts.append(starts[-1] + part.shape[0])

    def unpack(i):
        return wide_full[:, starts[i] : starts[i + 1]].reshape(-1, width_d)

    gate_full = jnp.concatenate([unpack(i) for i in range(ff_width)], axis=1)
    up_full = jnp.concatenate([unpack(ff_width + i) for i in range(ff_width)], axis=1)
    down_full = unpack(2 * ff_width)
    ssm_out_full = unpack(2 * ff_width + 1)
    attn_out_full = unpack(2 * ff_width + 2)
    z_full = unpack(2 * ff_width + 3).reshape(-1, z_proj.shape[1])
    q_width, k_width, v_width = q_proj.shape[1], k_proj.shape[1], v_proj.shape[1]
    q_at = xbc_proj.shape[1]
    k_at = q_at + q_width
    dt_at = k_at + k_width + v_width
    gain_at = dt_at + heads
    gain_one = rest_full[:, gain_at]
    gain_two = rest_full[:, gain_at + 1]
    ssm_gain_full = rest_full[:, gain_at + 2 : gain_at + 2 + gain_columns]
    ssm_gain_full = ssm_gain_full.reshape(-1, rows, gain_columns).transpose(0, 2, 1)
    ssm_gain_full = ssm_gain_full.reshape(-1, gain_columns * rows)[:, :gain_rows].reshape(-1)
    flat_tokens = tokens[0].astype(jnp.float32)
    normed, norm_one_back = jax.vjp(rms_apply, flat_tokens, gain_one.astype(jnp.float32))
    normed_b = normed.astype(jnp.bfloat16)
    rest_out = mat_dot(normed_b, rest_full)
    xbc_b = rest_out[:, :q_at].astype(jnp.bfloat16)
    gate_z = mat_dot(normed_b, z_full)
    query_b = rest_out[:, q_at:k_at].astype(jnp.bfloat16)
    kv_b = rest_out[:, k_at:dt_at].astype(jnp.bfloat16)
    dt_raw = rest_out[:, dt_at:gain_at]
    edge_rows = shift(xbc_b[tok_rows - pad_rows :], "seq", 1)
    xbc_ext = jnp.concatenate([edge_rows, xbc_b], axis=0).astype(jnp.float32)
    prepared, prep_back = jax.vjp(
        partial(ssm_prep, seg_ext=seg_ext),
        xbc_ext,
        dt_raw,
        conv_weight,
        conv_bias,
        dt_bias,
        decay_log,
    )
    ssm_input, b_input, c_input, step_size, log_decay = prepared
    state_parts, state_back = jax.vjp(
        partial(ssm_state, seg_here=seg_here, carry_last=carry_mask[-1]),
        ssm_input,
        b_input,
        step_size,
        log_decay,
    )
    passing, local_state = state_parts
    state_in = scan_states(passing, local_state, False)
    mixed, output_back = jax.vjp(
        partial(ssm_output, seg_here=seg_here, carry_mask=carry_mask),
        ssm_input,
        b_input,
        c_input,
        step_size,
        log_decay,
        state_in,
        gate_z,
        skip_gain,
        ssm_gain_full.astype(jnp.float32),
    )
    mixed_b = mixed.astype(jnp.bfloat16)
    kv_all = gather_seq(kv_b)
    kv_width = kv_b.shape[1] // 2
    keys_all, values_all = kv_all[:, :kv_width], kv_all[:, kv_width:]
    attended_b, log_total = attention_block(
        query_b, keys_all, values_all, query_pos, key_pos, seg_here, seg_row
    )
    resid = flat_tokens + mat_dot(mixed_b, ssm_out_full) + mat_dot(attended_b, attn_out_full)
    normed_two, norm_two_back = jax.vjp(rms_apply, resid, gain_two.astype(jnp.float32))
    normed_two_b = normed_two.astype(jnp.bfloat16)
    gate_val = mat_dot(normed_two_b, gate_full)
    up_val = mat_dot(normed_two_b, up_full)
    hidden, swiglu_back = jax.vjp(swiglu_mix, gate_val, up_val)
    hidden_b = hidden.astype(jnp.bfloat16)
    final = resid + mat_dot(hidden_b, down_full)
    block_out = final.astype(jnp.bfloat16)[None]
    cot_b = cotangent[0]
    cot_pair = both(cot_b)
    hidden_mine, hidden_other = pair_left(hidden_b, down_rows)
    hidden_pair = jnp.concatenate([hidden_mine, swap(hidden_other, 0)], 0)
    down_sum = Scatter(owners(row_contract(hidden_pair, cot_pair), down_rows), 2)
    hidden_grad = trans_dot(cot_b, down_full)
    gate_grad, up_grad = swiglu_back(hidden_grad)
    gate_grad_b = gate_grad.astype(jnp.bfloat16)
    up_grad_b = up_grad.astype(jnp.bfloat16)
    two_mine, two_other = pair_left(normed_two_b, rows)
    two_pair = jnp.concatenate([two_mine, swap(two_other, 0)], axis=0)
    gate_sum = Scatter(owners(row_contract(two_pair, both(gate_grad_b)), rows), 0)
    up_sum = Scatter(owners(row_contract(two_pair, both(up_grad_b)), rows), 1)
    normed_two_grad = trans_dot(gate_grad_b, gate_full) + trans_dot(up_grad_b, up_full)
    resid_norm_grad, second_gain_g = norm_two_back(normed_two_grad)
    resid_grad = cot_b.astype(jnp.float32) + resid_norm_grad
    resid_grad_b = resid_grad.astype(jnp.bfloat16)
    resid_pair = both(resid_grad_b)
    mixed_mine, mixed_other = pair_left(mixed_b, out_rows)
    att_mine, att_other = pair_left(attended_b, att_rows)
    outs_other = swap(jnp.concatenate([mixed_other, att_other], axis=1), 0)
    outs_pair = jnp.concatenate(
        [jnp.concatenate([mixed_mine, att_mine], axis=1), outs_other], axis=0
    )
    outs_g = row_contract(outs_pair, resid_pair)
    mixed_width = mixed_mine.shape[1]
    ssm_out_sum = Scatter(owners(outs_g[:mixed_width], out_rows), 0)
    attn_out_g = owners(outs_g[mixed_width:].astype(jnp.bfloat16), att_rows)
    attn_shape = attn_out_g.shape[:-2] + (rows, att_rows * width_d // rows)
    attn_out_g = attn_out_g.reshape(attn_shape)
    mixed_grad = trans_dot(resid_grad_b, ssm_out_full)
    attended_grad_b = trans_dot(resid_grad_b, attn_out_full).astype(jnp.bfloat16)
    (
        ga_input,
        ga_bvec,
        ga_cvec,
        ga_step,
        ga_decay,
        state_grad_local,
        z_grad,
        skip_gain_g,
        ssm_gain_g,
    ) = output_back(mixed_grad)
    ff = [gate_sum, up_sum, down_sum]
    state_grad_local, z_grad, attended_grad_b = advance(
        ff, state_grad_local, z_grad, attended_grad_b
    )
    z_grad_b = z_grad.astype(jnp.bfloat16)
    one_mine, one_other = pair_left(normed_b, rows)
    one_pair = jnp.concatenate([one_mine, swap(one_other, 0)], axis=0)
    z_attn_g = jnp.concatenate(
        [owners(row_contract(one_pair, both(z_grad_b)).astype(jnp.bfloat16), rows), attn_out_g],
        axis=-1,
    )
    z_attn_sum = Scatter(z_attn_g, 1)
    outs_sums = [ssm_out_sum, z_attn_sum]
    later_grad = scan_states(passing, state_grad_local, True)
    query_grad, key_part, value_part = attention_back(
        query_b,
        keys_all,
        values_all,
        attended_b,
        log_total,
        attended_grad_b,
        query_pos,
        key_pos,
        seg_here,
        seg_row,
    )
    query_grad, key_part, value_part = advance(
        ff + outs_sums, query_grad, key_part, value_part
    )
    kv_grad_b = scatter_seq(jnp.concatenate([key_part, value_part], axis=1), tok_rows).astype(
        jnp.bfloat16
    )
    passing_grad = jnp.sum(later_grad * state_in, axis=(1, 2))
    gb_input, gb_bvec, gb_step, gb_decay = state_back((passing_grad, later_grad))
    gb_step, gb_decay = advance(ff + outs_sums, gb_step, gb_decay)
    ext_grad, dt_raw_grad, conv_weight_g, conv_bias_g, dt_bias_g, decay_log_g = prep_back(
        (ga_input + gb_input, ga_bvec + gb_bvec, ga_cvec, ga_step + gb_step, ga_decay + gb_decay)
    )
    (dt_raw_grad,) = advance(ff + outs_sums, dt_raw_grad)
    gate_proj_g, up_proj_g, down_proj_g = gate_sum.result(), up_sum.result(), down_sum.result()
    edge_grad = shift(ext_grad[:pad_rows], "seq", -1)
    xbc_grad = ext_grad[pad_rows:] + jnp.concatenate(
        [jnp.zeros((tok_rows - pad_rows, ext_grad.shape[1]), jnp.float32), edge_grad], axis=0
    )
    xbc_grad_b = xbc_grad.astype(jnp.bfloat16)
    dt_grad_b = dt_raw_grad.astype(jnp.bfloat16)
    query_grad_b = query_grad.astype(jnp.bfloat16)
    rest_grad_b = jnp.concatenate(
        [xbc_grad_b, query_grad_b, kv_grad_b, dt_grad_b]
        + [jnp.zeros((tok_rows, rest_full.shape[1] - gain_at), jnp.bfloat16)],
        axis=1,
    )
    rest_g = owners(row_contract(one_pair, both(rest_grad_b)), rows).astype(jnp.bfloat16)
    rest_g, rest_grad_b = lax.optimization_barrier((rest_g, rest_grad_b))
    rest_sums = [Scatter(part, i) for i, part in enumerate(thirds(rest_g))]
    normed_grad = trans_dot(z_grad_b, z_full) + trans_dot(rest_grad_b, rest_full)
    token_norm_grad, first_gain_g = norm_one_back(normed_grad)
    tokens_grad = (resid_grad + token_norm_grad)[None]
    small = jnp.concatenate(
        [
            conv_weight_g.reshape(-1),
            conv_bias_g,
            first_gain_g,
            second_gain_g,
            ssm_gain_g,
            dt_bias_g,
            decay_log_g,
            skip_gain_g,
        ]
    )
    sizes = [conv_weight_g.size, conv_bias_g.size, width_d, width_d, ssm_gain_g.size]
    sizes = sizes + [heads, heads, heads]
    small = jnp.pad(small, (0, -small.size % 1024)).reshape(-1, 1024)
    for k in range(device_bits()):
        small = small + swap(small, k)
        if rest_sums[0].order:
            (small,) = advance(rest_sums, small)
    small = small.reshape(-1)
    z_attn_g, ssm_out_g = z_attn_sum.result(), ssm_out_sum.result()
    z_proj_g = z_attn_g[:, : z_proj.shape[1]]
    attn_out_g = z_attn_g[:, z_proj.shape[1] :].reshape(attn_out_proj.shape)
    rest_g = jnp.concatenate([part.result() for part in rest_sums], axis=1)
    xbc_proj_g = rest_g[:, :q_at]
    ends = [sum(sizes[: i + 1]) for i in range(len(sizes))]
    cw, cb, g1, g2, gs, db, dl, sk = [small[e - s : e] for s, e in zip(sizes, ends)]
    me = seq_rank * lax.axis_size("grp") + lax.axis_index("grp")

    def mine(whole, count):
        return lax.dynamic_slice_in_dim(whole, me * count, count)

    return (
        block_out,
        tokens_grad,
        mine(g1, rows),
        z_proj_g,
        xbc_proj_g,
        rest_g[:, dt_at:gain_at],
        cw.reshape(conv_weight_g.shape),
        cb,
        db,
        dl,
        sk,
        mine(gs, gain_rows),
        ssm_out_g,
        rest_g[:, q_at:k_at],
        rest_g[:, k_at : k_at + k_width],
        rest_g[:, k_at + k_width : dt_at],
        attn_out_g,
        mine(g2, rows),
        gate_proj_g,
        up_proj_g,
        down_proj_g,
    )


def solution(mesh):
    in_specs = (
        P("grp", "seq", None),
        P("grp", None),
        P("grp", "seq", None),
        P(("seq", "grp")),
        P(("seq", "grp"), None),
        P(("seq", "grp"), None),
        P(("seq", "grp"), None),
        P(),
        P(),
        P(),
        P(),
        P(),
        P(("seq", "grp")),
        P(("seq", "grp"), None),
        P(("seq", "grp"), None),
        P(("seq", "grp"), None),
        P(("seq", "grp"), None),
        P(("seq", "grp"), None),
        P(("seq", "grp")),
        P(("seq", "grp"), None),
        P(("seq", "grp"), None),
        P(("seq", "grp"), None),
    )
    out_specs = (
        P("grp", "seq", None),
        P("grp", "seq", None),
        P(("seq", "grp")),
        P(("seq", "grp"), None),
        P(("seq", "grp"), None),
        P(("seq", "grp"), None),
        P(),
        P(),
        P(),
        P(),
        P(),
        P(("seq", "grp")),
        P(("seq", "grp"), None),
        P(("seq", "grp"), None),
        P(("seq", "grp"), None),
        P(("seq", "grp"), None),
        P(("seq", "grp"), None),
        P(("seq", "grp")),
        P(("seq", "grp"), None),
        P(("seq", "grp"), None),
        P(("seq", "grp"), None),
    )
    return jax.shard_map(shards, mesh=mesh, in_specs=in_specs, out_specs=out_specs, check_vma=False)
```

```python
from functools import partial

import jax
import jax.numpy as jnp
from jax import lax
from jax.experimental import pallas as pl
from jax.experimental.pallas import tpu as pltpu
from jax.sharding import PartitionSpec as P

HEAD_DIM = 64
STATE = 128
CONV = 4
KV_HEADS = 2
ATT_DIM = 64
SSM_DIM = 1536


epsilon = 1e-05
att_scale = 0.125
highest = lax.Precision.DEFAULT


AXES = ("seq", "grp")


def shift(array, axis, by):
    length = lax.axis_size(axis)
    pairs = [(i, i + by) for i in range(length) if 0 <= i + by < length]
    return lax.ppermute(array, axis, pairs)


def device_count():
    return lax.axis_size("seq") * lax.axis_size("grp")


def device_bits():
    return device_count().bit_length() - 1


def device_bit(k):
    me = lax.axis_index("seq") * lax.axis_size("grp") + lax.axis_index("grp")
    return (me >> k) & 1


def swap(array, k):
    return lax.ppermute(array, AXES, [(i, i ^ (1 << k)) for i in range(device_count())])


def upward(array, k, down):
    senders = [i for i in range(device_count()) if ((i >> k) & 1) == (1 if down else 0)]
    return lax.ppermute(array, AXES, [(i, i ^ (1 << k)) for i in senders])


def order_of(color):
    bits = device_bits()
    low = list(range(1, bits - 1))
    by = color * len(low) // 3
    return low[by:] + low[:by] + [bits - 1]


def double(array, k, dim):
    other = swap(array, k)
    bit = device_bit(k)
    low = jnp.where(bit == 0, array, other)
    high = jnp.where(bit == 0, other, array)
    return jnp.concatenate([low, high], axis=dim)


def halve(array, k, dim):
    bit = device_bit(k)
    keep = lax.dynamic_index_in_dim(array, bit, dim, keepdims=True)
    send = lax.dynamic_index_in_dim(array, 1 - bit, dim, keepdims=True)
    return keep.astype(jnp.float32) + swap(send, k).astype(jnp.float32)


def gather_rows(piece, color):
    bits = device_bits()
    rows, width = piece.shape
    array = piece.reshape((1,) * bits + (rows, width))
    for k in order_of(color)[::-1] + [0]:
        array = double(array, k, bits - 1 - k)
    return array.reshape(device_count() * rows, width)


class Scatter:
    def __init__(self, array, color):
        self.array = array.astype(jnp.bfloat16)
        self.order = order_of(color)

    def start(self):
        k = self.order.pop(0)
        dim, bit = device_bits() - 1 - k, device_bit(k)
        keep = lax.dynamic_index_in_dim(self.array, bit, dim, keepdims=True)
        send = lax.dynamic_index_in_dim(self.array, 1 - bit, dim, keepdims=True)
        return keep, swap(send, k)

    def finish(self, pending):
        keep, received = pending
        self.array = keep.astype(jnp.float32) + received.astype(jnp.float32)
        if self.order:
            self.array = self.array.astype(jnp.bfloat16)

    def result(self):
        while self.order:
            self.finish(self.start())
        return self.array.reshape(self.array.shape[-2:])


def advance(scatters, *others):
    pending = [scatter.start() for scatter in scatters]
    pending, others = lax.optimization_barrier((pending, others))
    for scatter, item in zip(scatters, pending):
        scatter.finish(item)
    return others


def seq_bits():
    return lax.axis_size("seq").bit_length() - 1


def gather_seq(array):
    bits = seq_bits()
    base = device_bits() - bits
    rows, width = array.shape
    array = array.reshape((1,) * bits + (rows, width))
    for k in range(bits):
        array = double(array, base + k, bits - 1 - k)
    return array.reshape(-1, width)


def scatter_seq(array, rows):
    bits = seq_bits()
    base = device_bits() - bits
    array = array.reshape((2,) * bits + (rows, array.shape[-1]))
    for k in range(bits):
        array = halve(array.astype(jnp.bfloat16), base + k, bits - 1 - k)
    return array.reshape(rows, -1)


def own_half(array, rows, which):
    parts = array.reshape(array.shape[0], -1, 2, rows, *array.shape[2:])
    return lax.dynamic_index_in_dim(parts, which, 2, keepdims=False).reshape(array.shape[0], -1)


def pair_left(array, rows):
    bit = device_bit(0)
    mine = own_half(array, rows, bit)
    return mine, own_half(array, rows, 1 - bit)


def both(array):
    return jnp.concatenate([array, swap(array, 0)], axis=0)


def owners(array, rows):
    return array.reshape((2,) * (device_bits() - 1) + (1, rows, array.shape[-1]))


def thirds(array):
    width = array.shape[-1]
    step = -(-width // (3 * 128)) * 128
    return [array[..., i : min(i + step, width)] for i in range(0, width, step)]


def scan_states(decay, local, down):
    bits = seq_bits()
    base = device_bits() - bits
    heads, rows, width = local.shape

    def pack(decay, state):
        high = lax.reduce_precision(decay, 8, 7)
        low = decay - high
        extra = jnp.zeros((16, width), jnp.float32).at[0, :heads].set(high).at[1, :heads].set(low)
        return jnp.concatenate(
            [state.reshape(-1, width).astype(jnp.bfloat16), extra.astype(jnp.bfloat16)], axis=0
        )

    def unpack(buffer):
        wide = buffer.astype(jnp.float32)
        decay = wide[heads * rows, :heads] + wide[heads * rows + 1, :heads]
        return decay, wide[: heads * rows].reshape(heads, rows, width)

    ahead = (jnp.ones_like(decay), jnp.zeros_like(local))
    total = (decay, local)
    for k in range(bits):
        bit = device_bit(base + k)
        later = (bit == 0) if down else (bit == 1)
        buffer = pack(*total)
        last = k == bits - 1
        received = unpack(upward(buffer, base + k, down) if last else swap(buffer, base + k))
        joined = state_combine(received, ahead)
        ahead = jax.tree.map(lambda a, b: jnp.where(later, a, b), joined, ahead)
        if not last:
            first = jax.tree.map(lambda a, b: jnp.where(later, a, b), received, total)
            second = jax.tree.map(lambda a, b: jnp.where(later, b, a), received, total)
            total = state_combine(first, second)
    return ahead[1]


def unpack_kernel(moves, source, *results):
    for result, row, height, col, width, to_row, to_col in moves:
        value = source[:, row : row + height, col : col + width]
        results[result][:, to_row : to_row + height, to_col : to_col + width] = value


def unpack_rows(packed, shapes, moves):
    count = packed.shape[0]
    step = 2
    return [
        r.reshape(-1, r.shape[-1])
        for r in pl.pallas_call(
            partial(unpack_kernel, moves),
            out_shape=[jax.ShapeDtypeStruct((count, *shape), jnp.bfloat16) for shape in shapes],
            grid=(count // step,),
            in_specs=[pl.BlockSpec((step, *packed.shape[1:]), lambda b: (b, 0, 0))],
            out_specs=[pl.BlockSpec((step, *shape), lambda b: (b, 0, 0)) for shape in shapes],
            cost_estimate=pl.CostEstimate(
                flops=0, bytes_accessed=4 * packed.size, transcendentals=0
            ),
        )(packed)
    ]


def rms_apply(values, gain):
    inverse = lax.rsqrt(jnp.mean(values * values, axis=-1, keepdims=True) + epsilon)
    return values * inverse * gain


def mat_dot(left, right):
    return jnp.dot(left, right, preferred_element_type=jnp.float32)


def trans_dot(left, right):
    return lax.dot_general(
        left, right, (((1,), (1,)), ((), ())), preferred_element_type=jnp.float32
    )


def row_contract(left, right):
    return lax.dot_general(
        left, right, (((0,), (0,)), ((), ())), preferred_element_type=jnp.float32
    )


def swiglu_mix(gate_in, up_in):
    return jax.nn.silu(gate_in) * up_in


def state_combine(earlier, later):
    return (earlier[0] * later[0], later[0][:, None, None] * earlier[1] + later[1])


def ssm_prep(xbc_ext, dt_raw, conv_weight, conv_bias, dt_bias, decay_log, seg_ext):
    tok_rows = dt_raw.shape[0]
    seg_here = seg_ext[CONV - 1 :]
    conv_total = jnp.zeros((tok_rows, xbc_ext.shape[1]), jnp.float32) + conv_bias[None, :]
    for lag_index in range(CONV):
        shifted = xbc_ext[lag_index : lag_index + tok_rows]
        same_seg = seg_ext[lag_index : lag_index + tok_rows] == seg_here
        conv_total = (
            conv_total
            + jnp.where(same_seg[:, None], shifted, 0.0) * conv_weight[lag_index][None, :]
        )
    activated = jax.nn.silu(conv_total)
    ssm_input = activated[:, :SSM_DIM]
    b_input = activated[:, SSM_DIM : SSM_DIM + STATE]
    c_input = activated[:, SSM_DIM + STATE :]
    step_size = jax.nn.softplus(dt_raw + dt_bias[None, :])
    log_decay = -step_size * jnp.exp(decay_log)[None, :]
    return (ssm_input, b_input, c_input, step_size, log_decay)


def ssm_output(
    ssm_input,
    b_input,
    c_input,
    step_size,
    log_decay,
    state_in,
    gate_z,
    skip_gain,
    ssm_gain,
    seg_here,
    carry_mask,
):
    tok_rows, head_count = step_size.shape
    inputs_h = ssm_input.reshape(tok_rows, head_count, HEAD_DIM)
    cumulative = jnp.cumsum(log_decay, axis=0)
    positions = jnp.arange(tok_rows)
    allowed = (seg_here[:, None] == seg_here[None, :]) & (positions[:, None] >= positions[None, :])
    allowed_h = allowed[:, :, None]
    spread = cumulative[:, None, :] - cumulative[None, :, :]
    weights_h = jnp.where(allowed_h, jnp.exp(jnp.where(allowed_h, spread, 0.0)), 0.0)
    intersection = jnp.dot(c_input, b_input.T, precision=highest)
    mixing = weights_h * intersection[:, :, None] * step_size[None, :, :]
    within = jnp.einsum("tsh,shp->thp", mixing, inputs_h, precision=highest)
    carried = jnp.einsum("tn,hpn->thp", c_input, state_in, precision=highest)
    carried = carried * (jnp.exp(cumulative) * carry_mask[:, None])[:, :, None]
    outputs_h = within + carried + skip_gain[None, :, None] * inputs_h
    gated = outputs_h.reshape(tok_rows, -1) * jax.nn.silu(gate_z)
    return rms_apply(gated, ssm_gain)


def ssm_state(ssm_input, b_input, step_size, log_decay, seg_here, carry_last):
    tok_rows, head_count = step_size.shape
    inputs_h = ssm_input.reshape(tok_rows, head_count, HEAD_DIM)
    cumulative = jnp.cumsum(log_decay, axis=0)
    final_sum = cumulative[-1]
    same_last = (seg_here == seg_here[-1]).astype(jnp.float32)
    weighting = jnp.exp(final_sum[None, :] - cumulative) * step_size * same_last[:, None]
    local_state = jnp.einsum("th,thp,tn->hpn", weighting, inputs_h, b_input, precision=highest)
    passing = jnp.exp(final_sum) * carry_last
    return (passing, local_state)


def attention_block(query_b, keys_b, values_b, query_pos, key_pos, query_seg, key_seg):
    q_rows = query_b.shape[0]
    k_rows = keys_b.shape[0]
    group = query_b.shape[1] // (KV_HEADS * ATT_DIM)
    query_h = query_b.reshape(q_rows, KV_HEADS, group, ATT_DIM)
    key_h = keys_b.reshape(k_rows, KV_HEADS, ATT_DIM)
    value_h = values_b.reshape(k_rows, KV_HEADS, ATT_DIM)
    scores = (
        jnp.einsum("rkgd,ckd->kgrc", query_h, key_h, preferred_element_type=jnp.float32) * att_scale
    )
    allowed = (key_pos[None, :] <= query_pos[:, None]) & (key_seg[None, :] == query_seg[:, None])
    scores = jnp.where(allowed[None, None], scores, -1e30)
    top_score = jnp.max(scores, axis=-1, keepdims=True)
    total = jnp.sum(jnp.exp(scores - top_score), axis=-1, keepdims=True)
    log_total = top_score + jnp.log(total)
    probs_b = jnp.exp(scores - log_total).astype(jnp.bfloat16)
    output = jnp.einsum("kgrc,ckd->rkgd", probs_b, value_h, preferred_element_type=jnp.float32)
    return (output.reshape(q_rows, -1).astype(jnp.bfloat16), log_total[..., 0])


def attention_back(
    query_b, keys_b, values_b, out_b, log_total, grad_b, query_pos, key_pos, query_seg, key_seg
):
    q_rows = query_b.shape[0]
    k_rows = keys_b.shape[0]
    group = query_b.shape[1] // (KV_HEADS * ATT_DIM)
    query_h = query_b.reshape(q_rows, KV_HEADS, group, ATT_DIM)
    key_h = keys_b.reshape(k_rows, KV_HEADS, ATT_DIM)
    value_h = values_b.reshape(k_rows, KV_HEADS, ATT_DIM)
    grad_h = grad_b.reshape(q_rows, KV_HEADS, group, ATT_DIM)
    out_h = out_b.reshape(q_rows, KV_HEADS, group, ATT_DIM)
    scores = (
        jnp.einsum("rkgd,ckd->kgrc", query_h, key_h, preferred_element_type=jnp.float32) * att_scale
    )
    allowed = (key_pos[None, :] <= query_pos[:, None]) & (key_seg[None, :] == query_seg[:, None])
    scores = jnp.where(allowed[None, None], scores, -1e30)
    probs = jnp.exp(scores - log_total[..., None])
    probs_b = probs.astype(jnp.bfloat16)
    delta = jnp.transpose(
        jnp.sum(grad_h.astype(jnp.float32) * out_h.astype(jnp.float32), axis=-1), (1, 2, 0)
    )
    prob_grad = jnp.einsum("rkgd,ckd->kgrc", grad_h, value_h, preferred_element_type=jnp.float32)
    score_grad = (probs * (prob_grad - delta[..., None]) * att_scale).astype(jnp.bfloat16)
    query_grad = jnp.einsum(
        "kgrc,ckd->rkgd", score_grad, key_h, preferred_element_type=jnp.float32
    ).reshape(q_rows, -1)
    key_grad = jnp.einsum(
        "kgrc,rkgd->ckd", score_grad, query_h, preferred_element_type=jnp.float32
    ).reshape(k_rows, -1)
    value_grad = jnp.einsum(
        "kgrc,rkgd->ckd", probs_b, grad_h, preferred_element_type=jnp.float32
    ).reshape(k_rows, -1)
    return (query_grad, key_grad, value_grad)


def shards(
    tokens,
    segment_ids,
    cotangent,
    first_gain,
    z_proj,
    xbc_proj,
    dt_proj,
    conv_weight,
    conv_bias,
    dt_bias,
    decay_log,
    skip_gain,
    ssm_gain,
    ssm_out_proj,
    q_proj,
    k_proj,
    v_proj,
    attn_out_proj,
    second_gain,
    gate_proj,
    up_proj,
    down_proj,
):
    seq_rank = lax.axis_index("seq")
    tok_rows = tokens.shape[1]
    length = segment_ids.shape[1]
    pad_rows = CONV - 1
    row_start = seq_rank * tok_rows
    seg_row = segment_ids[0]
    seg_padded = jnp.concatenate([jnp.full((pad_rows,), -1, jnp.int32), seg_row], axis=0)
    seg_ext = lax.dynamic_slice_in_dim(seg_padded, row_start, tok_rows + pad_rows)
    seg_here = seg_ext[pad_rows:]
    carry_mask = (seg_here == seg_ext[pad_rows - 1]).astype(jnp.float32)
    query_pos = row_start + jnp.arange(tok_rows)
    key_pos = jnp.arange(length)
    rows = z_proj.shape[0]
    out_rows, att_rows, down_rows = ssm_out_proj.shape[0], attn_out_proj.shape[0], down_proj.shape[0]
    width_d = tokens.shape[2]
    bc_width = xbc_proj.shape[1] - SSM_DIM
    gain_rows = ssm_gain.shape[0]
    gain_columns = -(-gain_rows // rows)
    heads = dt_proj.shape[1]
    ssm_gain_cols = jnp.pad(ssm_gain, (0, gain_columns * rows - gain_rows)).reshape(
        gain_columns, rows
    )
    tail_parts = [dt_proj, first_gain[:, None], second_gain[:, None], ssm_gain_cols.T]
    tail_width = sum(part.shape[1] for part in tail_parts)
    tail_pad = -tail_width % 128
    rest = jnp.concatenate(
        [xbc_proj, q_proj, k_proj, v_proj, *tail_parts]
        + [jnp.zeros((rows, tail_pad), z_proj.dtype)],
        axis=1,
    )
    ff_width = gate_proj.shape[1] // width_d
    wide = [gate_proj[:, i * width_d : (i + 1) * width_d] for i in range(ff_width)]
    wide = wide + [up_proj[:, i * width_d : (i + 1) * width_d] for i in range(ff_width)]
    half = rows // 2
    z_left, z_right = z_proj[:, :width_d], z_proj[:, width_d:]
    z_right = jnp.concatenate([z_right[:half], z_right[half:]], axis=1)
    wide = wide + [down_proj, ssm_out_proj, attn_out_proj, z_left, z_right]
    wide_full = lax.all_gather(jnp.concatenate(wide, axis=0), AXES)
    rest_full = jnp.concatenate(
        [gather_rows(part, i) for i, part in enumerate(thirds(rest))], axis=1
    )
    wide_shapes = [gate_proj.shape, up_proj.shape, down_proj.shape]
    wide_shapes += [ssm_out_proj.shape, attn_out_proj.shape, z_proj.shape]
    places = [(0, i * width_d) for i in range(ff_width)] + [(1, i * width_d) for i in range(ff_width)]
    places += [(2, 0), (3, 0), (4, 0), (5, 0)]
    wide_moves, at = [], 0
    for part, (result, col) in zip(wide, places):
        wide_moves.append((result, at, part.shape[0], 0, width_d, 0, col))
        at += part.shape[0]
    right = z_right.shape[1] // 2
    wide_moves.append((5, at, half, 0, right, 0, width_d))
    wide_moves.append((5, at, half, right, right, half, width_d))
    gate_full, up_full, down_full, ssm_out_full, attn_out_full, z_full = unpack_rows(
        wide_full, wide_shapes, wide_moves
    )
    q_width, k_width, v_width = q_proj.shape[1], k_proj.shape[1], v_proj.shape[1]
    q_at = xbc_proj.shape[1]
    k_at = q_at + q_width
    dt_at = k_at + k_width + v_width
    gain_at = dt_at + heads
    gain_one = rest_full[:, gain_at]
    gain_two = rest_full[:, gain_at + 1]
    ssm_gain_full = rest_full[:, gain_at + 2 : gain_at + 2 + gain_columns]
    ssm_gain_full = ssm_gain_full.reshape(-1, rows, gain_columns).transpose(0, 2, 1)
    ssm_gain_full = ssm_gain_full.reshape(-1, gain_columns * rows)[:, :gain_rows].reshape(-1)
    flat_tokens = tokens[0].astype(jnp.float32)
    normed, norm_one_back = jax.vjp(rms_apply, flat_tokens, gain_one.astype(jnp.float32))
    normed_b = normed.astype(jnp.bfloat16)
    rest_out = mat_dot(normed_b, rest_full)
    xbc_b = rest_out[:, :q_at].astype(jnp.bfloat16)
    gate_z = mat_dot(normed_b, z_full)
    query_b = rest_out[:, q_at:k_at].astype(jnp.bfloat16)
    kv_b = rest_out[:, k_at:dt_at].astype(jnp.bfloat16)
    dt_raw = rest_out[:, dt_at:gain_at]
    edge_rows = shift(xbc_b[tok_rows - pad_rows :], "seq", 1)
    xbc_ext = jnp.concatenate([edge_rows, xbc_b], axis=0).astype(jnp.float32)
    prepared, prep_back = jax.vjp(
        partial(ssm_prep, seg_ext=seg_ext),
        xbc_ext,
        dt_raw,
        conv_weight,
        conv_bias,
        dt_bias,
        decay_log,
    )
    ssm_input, b_input, c_input, step_size, log_decay = prepared
    state_parts, state_back = jax.vjp(
        partial(ssm_state, seg_here=seg_here, carry_last=carry_mask[-1]),
        ssm_input,
        b_input,
        step_size,
        log_decay,
    )
    passing, local_state = state_parts
    state_in = scan_states(passing, local_state, False)
    mixed, output_back = jax.vjp(
        partial(ssm_output, seg_here=seg_here, carry_mask=carry_mask),
        ssm_input,
        b_input,
        c_input,
        step_size,
        log_decay,
        state_in,
        gate_z,
        skip_gain,
        ssm_gain_full.astype(jnp.float32),
    )
    mixed_b = mixed.astype(jnp.bfloat16)
    kv_all = gather_seq(kv_b)
    kv_width = kv_b.shape[1] // 2
    keys_all, values_all = kv_all[:, :kv_width], kv_all[:, kv_width:]
    attended_b, log_total = attention_block(
        query_b, keys_all, values_all, query_pos, key_pos, seg_here, seg_row
    )
    resid = flat_tokens + mat_dot(mixed_b, ssm_out_full) + mat_dot(attended_b, attn_out_full)
    normed_two, norm_two_back = jax.vjp(rms_apply, resid, gain_two.astype(jnp.float32))
    normed_two_b = normed_two.astype(jnp.bfloat16)
    gate_val = mat_dot(normed_two_b, gate_full)
    up_val = mat_dot(normed_two_b, up_full)
    hidden, swiglu_back = jax.vjp(swiglu_mix, gate_val, up_val)
    hidden_b = hidden.astype(jnp.bfloat16)
    final = resid + mat_dot(hidden_b, down_full)
    block_out = final.astype(jnp.bfloat16)[None]
    cot_b = cotangent[0]
    cot_pair = both(cot_b)
    hidden_mine, hidden_other = pair_left(hidden_b, down_rows)
    hidden_pair = jnp.concatenate([hidden_mine, swap(hidden_other, 0)], 0)
    down_sum = Scatter(owners(row_contract(hidden_pair, cot_pair), down_rows), 2)
    hidden_grad = trans_dot(cot_b, down_full)
    gate_grad, up_grad = swiglu_back(hidden_grad)
    gate_grad_b = gate_grad.astype(jnp.bfloat16)
    up_grad_b = up_grad.astype(jnp.bfloat16)
    two_mine, two_other = pair_left(normed_two_b, rows)
    two_pair = jnp.concatenate([two_mine, swap(two_other, 0)], axis=0)
    gate_sum = Scatter(owners(row_contract(two_pair, both(gate_grad_b)), rows), 0)
    up_sum = Scatter(owners(row_contract(two_pair, both(up_grad_b)), rows), 1)
    normed_two_grad = trans_dot(gate_grad_b, gate_full) + trans_dot(up_grad_b, up_full)
    resid_norm_grad, second_gain_g = norm_two_back(normed_two_grad)
    resid_grad = cot_b.astype(jnp.float32) + resid_norm_grad
    resid_grad_b = resid_grad.astype(jnp.bfloat16)
    resid_pair = both(resid_grad_b)
    mixed_mine, mixed_other = pair_left(mixed_b, out_rows)
    att_mine, att_other = pair_left(attended_b, att_rows)
    outs_other = swap(jnp.concatenate([mixed_other, att_other], axis=1), 0)
    outs_pair = jnp.concatenate(
        [jnp.concatenate([mixed_mine, att_mine], axis=1), outs_other], axis=0
    )
    outs_g = row_contract(outs_pair, resid_pair)
    mixed_width = mixed_mine.shape[1]
    ssm_out_sum = Scatter(owners(outs_g[:mixed_width], out_rows), 0)
    attn_out_g = owners(outs_g[mixed_width:].astype(jnp.bfloat16), att_rows)
    attn_shape = attn_out_g.shape[:-2] + (rows, att_rows * width_d // rows)
    attn_out_g = attn_out_g.reshape(attn_shape)
    mixed_grad = trans_dot(resid_grad_b, ssm_out_full)
    attended_grad_b = trans_dot(resid_grad_b, attn_out_full).astype(jnp.bfloat16)
    (
        ga_input,
        ga_bvec,
        ga_cvec,
        ga_step,
        ga_decay,
        state_grad_local,
        z_grad,
        skip_gain_g,
        ssm_gain_g,
    ) = output_back(mixed_grad)
    ff = [gate_sum, up_sum, down_sum]
    state_grad_local, z_grad, attended_grad_b = advance(
        ff, state_grad_local, z_grad, attended_grad_b
    )
    z_grad_b = z_grad.astype(jnp.bfloat16)
    one_mine, one_other = pair_left(normed_b, rows)
    one_pair = jnp.concatenate([one_mine, swap(one_other, 0)], axis=0)
    z_attn_g = jnp.concatenate(
        [owners(row_contract(one_pair, both(z_grad_b)).astype(jnp.bfloat16), rows), attn_out_g],
        axis=-1,
    )
    z_attn_sum = Scatter(z_attn_g, 1)
    outs_sums = [ssm_out_sum, z_attn_sum]
    later_grad = scan_states(passing, state_grad_local, True)
    query_grad, key_part, value_part = attention_back(
        query_b,
        keys_all,
        values_all,
        attended_b,
        log_total,
        attended_grad_b,
        query_pos,
        key_pos,
        seg_here,
        seg_row,
    )
    query_grad, key_part, value_part = advance(
        ff + outs_sums, query_grad, key_part, value_part
    )
    kv_grad_b = scatter_seq(jnp.concatenate([key_part, value_part], axis=1), tok_rows).astype(
        jnp.bfloat16
    )
    passing_grad = jnp.sum(later_grad * state_in, axis=(1, 2))
    gb_input, gb_bvec, gb_step, gb_decay = state_back((passing_grad, later_grad))
    gb_step, gb_decay = advance(ff + outs_sums, gb_step, gb_decay)
    ext_grad, dt_raw_grad, conv_weight_g, conv_bias_g, dt_bias_g, decay_log_g = prep_back(
        (ga_input + gb_input, ga_bvec + gb_bvec, ga_cvec, ga_step + gb_step, ga_decay + gb_decay)
    )
    (dt_raw_grad,) = advance(ff + outs_sums, dt_raw_grad)
    gate_proj_g, up_proj_g, down_proj_g = gate_sum.result(), up_sum.result(), down_sum.result()
    edge_grad = shift(ext_grad[:pad_rows], "seq", -1)
    xbc_grad = ext_grad[pad_rows:] + jnp.concatenate(
        [jnp.zeros((tok_rows - pad_rows, ext_grad.shape[1]), jnp.float32), edge_grad], axis=0
    )
    xbc_grad_b = xbc_grad.astype(jnp.bfloat16)
    dt_grad_b = dt_raw_grad.astype(jnp.bfloat16)
    query_grad_b = query_grad.astype(jnp.bfloat16)
    rest_grad_b = jnp.concatenate(
        [xbc_grad_b, query_grad_b, kv_grad_b, dt_grad_b]
        + [jnp.zeros((tok_rows, rest_full.shape[1] - gain_at), jnp.bfloat16)],
        axis=1,
    )
    rest_g = owners(row_contract(one_pair, both(rest_grad_b)), rows).astype(jnp.bfloat16)
    rest_g, rest_grad_b = lax.optimization_barrier((rest_g, rest_grad_b))
    rest_sums = [Scatter(part, i) for i, part in enumerate(thirds(rest_g))]
    normed_grad = trans_dot(z_grad_b, z_full) + trans_dot(rest_grad_b, rest_full)
    token_norm_grad, first_gain_g = norm_one_back(normed_grad)
    tokens_grad = (resid_grad + token_norm_grad)[None]
    small = jnp.concatenate(
        [
            conv_weight_g.reshape(-1),
            conv_bias_g,
            first_gain_g,
            second_gain_g,
            ssm_gain_g,
            dt_bias_g,
            decay_log_g,
            skip_gain_g,
        ]
    )
    sizes = [conv_weight_g.size, conv_bias_g.size, width_d, width_d, ssm_gain_g.size]
    sizes = sizes + [heads, heads, heads]
    small = jnp.pad(small, (0, -small.size % 1024)).reshape(-1, 1024)
    for k in range(device_bits()):
        small = small + swap(small, k)
        if rest_sums[0].order:
            (small,) = advance(rest_sums, small)
    small = small.reshape(-1)
    z_attn_g, ssm_out_g = z_attn_sum.result(), ssm_out_sum.result()
    z_proj_g = z_attn_g[:, : z_proj.shape[1]]
    attn_out_g = z_attn_g[:, z_proj.shape[1] :].reshape(attn_out_proj.shape)
    rest_g = jnp.concatenate([part.result() for part in rest_sums], axis=1)
    xbc_proj_g = rest_g[:, :q_at]
    ends = [sum(sizes[: i + 1]) for i in range(len(sizes))]
    cw, cb, g1, g2, gs, db, dl, sk = [small[e - s : e] for s, e in zip(sizes, ends)]
    me = seq_rank * lax.axis_size("grp") + lax.axis_index("grp")

    def mine(whole, count):
        return lax.dynamic_slice_in_dim(whole, me * count, count)

    return (
        block_out,
        tokens_grad,
        mine(g1, rows),
        z_proj_g,
        xbc_proj_g,
        rest_g[:, dt_at:gain_at],
        cw.reshape(conv_weight_g.shape),
        cb,
        db,
        dl,
        sk,
        mine(gs, gain_rows),
        ssm_out_g,
        rest_g[:, q_at:k_at],
        rest_g[:, k_at : k_at + k_width],
        rest_g[:, k_at + k_width : dt_at],
        attn_out_g,
        mine(g2, rows),
        gate_proj_g,
        up_proj_g,
        down_proj_g,
    )


def solution(mesh):
    in_specs = (
        P("grp", "seq", None),
        P("grp", None),
        P("grp", "seq", None),
        P(("seq", "grp")),
        P(("seq", "grp"), None),
        P(("seq", "grp"), None),
        P(("seq", "grp"), None),
        P(),
        P(),
        P(),
        P(),
        P(),
        P(("seq", "grp")),
        P(("seq", "grp"), None),
        P(("seq", "grp"), None),
        P(("seq", "grp"), None),
        P(("seq", "grp"), None),
        P(("seq", "grp"), None),
        P(("seq", "grp")),
        P(("seq", "grp"), None),
        P(("seq", "grp"), None),
        P(("seq", "grp"), None),
    )
    out_specs = (
        P("grp", "seq", None),
        P("grp", "seq", None),
        P(("seq", "grp")),
        P(("seq", "grp"), None),
        P(("seq", "grp"), None),
        P(("seq", "grp"), None),
        P(),
        P(),
        P(),
        P(),
        P(),
        P(("seq", "grp")),
        P(("seq", "grp"), None),
        P(("seq", "grp"), None),
        P(("seq", "grp"), None),
        P(("seq", "grp"), None),
        P(("seq", "grp"), None),
        P(("seq", "grp")),
        P(("seq", "grp"), None),
        P(("seq", "grp"), None),
        P(("seq", "grp"), None),
    )
    return jax.shard_map(shards, mesh=mesh, in_specs=in_specs, out_specs=out_specs, check_vma=False)
```
